32 devices in a mesh: parts: 2 (over y), seq: 4 (over z), head: 4 (over x, core).
Axes of the slice: x: 2, y: 2, z: 4, core: 2. Of those that a mesh axis runs over, the one named last changes fastest.
Arguments:
- queries: bfloat16 [2048, 16, 128], P(('parts', 'seq'), 'head'), parts along dimension 0, may hold values from -6 to 6
- keys: bfloat16 [2048, 16, 128], P(('parts', 'seq'), 'head'), parts along dimension 0, may hold values from -8 to 8
- values: bfloat16 [2048, 16, 128], P(('parts', 'seq'), 'head'), parts along dimension 0, may hold values from -6 to 6
- delta_keys: bfloat16 [2048, 2, 16, 128], P(('parts', 'seq'), None, 'head'), parts along dimension 0, may hold values from -6 to 6
- delta_values: bfloat16 [2048, 2, 16, 128], P(('parts', 'seq'), None, 'head'), parts along dimension 0, may hold values from -6 to 6
- betas: float32 [2, 16, 2048], P(None, 'head', ('parts', 'seq')), parts along dimension 2, may hold values from 0.2 to 1.8
- decays: float32 [16, 2048], P('head', ('parts', 'seq')), parts along dimension 1, may hold values from 0.4 to 1
- grad_out: bfloat16 [2048, 16, 128], P(('parts', 'seq'), 'head'), parts along dimension 0, may hold values from -6 to 6
Outputs:
- grad_queries: bfloat16 [2048, 16, 128], P(('parts', 'seq'), 'head'), parts along dimension 0
- grad_keys: bfloat16 [2048, 16, 128], P(('parts', 'seq'), 'head'), parts along dimension 0
- grad_values: bfloat16 [2048, 16, 128], P(('parts', 'seq'), 'head'), parts along dimension 0
- grad_delta_keys: bfloat16 [2048, 2, 16, 128], P(('parts', 'seq'), None, 'head'), parts along dimension 0
- grad_delta_values: bfloat16 [2048, 2, 16, 128], P(('parts', 'seq'), None, 'head'), parts along dimension 0
- grad_betas: float32 [2, 16, 2048], P(None, 'head', ('parts', 'seq')), parts along dimension 2
- grad_decays: float32 [16, 2048], P('head', ('parts', 'seq')), parts along dimension 1
The draws below stay inside these ranges and needn't reach their ends.
There are 2 independent parts, one for each index of `parts`. The reference program is written for one: setup_inputs(seed, part) draws one part's arguments, and reference() takes and returns one part's arrays. A program takes and returns all parts, laid end to end along the dimension named above; each array names one. Nothing has to cross between parts.
All inputs are finite; a program needn't handle non-finite values.
Results may differ from the reference program's by a relative error of at most 0.02.
Values may be sent and summed in bfloat16 or wider, within the bound.
No kernel may reach another device: no remote copies, remote signals or barrier semaphores. Data moves between devices by JAX's collectives and lax.ppermute only.
A program may use at most 128 MiB of HBM per device.

```python
import math
import jax
import jax.numpy as jnp
from jax import lax

HEAD_COUNT = 16
E = 128
WINDOW = 1024
SEQUENCE_LENGTH = 1024


def drawn_pair(key):
    base = jax.random.fold_in(key, 11)
    first, second = jax.random.split(base, 2)
    shape = (SEQUENCE_LENGTH, HEAD_COUNT, E)
    query_vals = jnp.clip(jax.random.normal(first, shape, jnp.float32), -6.0, 6.0)
    key_vals = jnp.clip(jax.random.normal(second, shape, jnp.float32), -6.0, 6.0)
    return (query_vals, key_vals)


def draw_queries(key, part):
    return drawn_pair(key)[0].astype(jnp.bfloat16)


def draw_keys(key, part):
    return drawn_pair(key)[1].astype(jnp.bfloat16)


def draw_decays(key, part):
    first, second, third, fourth_part, fifth = jax.random.split(jax.random.fold_in(key, 23), 5)
    share = 0.5
    pick = jax.random.uniform(first, (HEAD_COUNT, 1), jnp.float32)
    reach = jax.random.uniform(second, (HEAD_COUNT, 1), jnp.float32, 30.0, 50.0)
    fast_rate = math.log(0.1) / reach
    slow_rate = math.log(0.5) / SEQUENCE_LENGTH
    decay_rate = jnp.where(pick < share, fast_rate, slow_rate)
    random_jitter = jax.random.uniform(third, (HEAD_COUNT, SEQUENCE_LENGTH), jnp.float32, 0.5, 2.0)
    spike_amount = jax.random.uniform(fourth_part, (HEAD_COUNT, SEQUENCE_LENGTH), jnp.float32) < 2.0 / SEQUENCE_LENGTH
    scale_factor = jax.random.uniform(fifth, (HEAD_COUNT, SEQUENCE_LENGTH), jnp.float32, 0.5, 0.8)
    return jnp.exp(decay_rate * random_jitter) * jnp.where(spike_amount, scale_factor, 1.0)


def shard_levels(rng, dims, pieces, smallest, largest):
    gain, own = 1.0, jax.random.fold_in(rng, 6)
    for axis_at, shards_of in pieces:
        heights = jnp.exp(jax.random.uniform(jax.random.fold_in(own, axis_at), (shards_of,), jnp.float32, smallest / len(pieces), largest / len(pieces)))
        gain = gain * jnp.repeat(heights, dims[axis_at] // shards_of).reshape([-1 if axis == axis_at else 1 for axis in range(len(dims))])
    return gain


def centred(stream_key, dims, scale, most, cuts=(), held_as=jnp.bfloat16):
    result = jax.random.normal(stream_key, dims, jnp.float32) * scale
    if len(cuts) > 0:
        result = shard_levels(stream_key, dims, cuts, -0.22, 0.18) * result
    return jnp.clip(result, min=-most, max=most).astype(held_as)


def setup_inputs(seed: int = 0, part: int = 0) -> dict:
    splits = jax.random.split(jax.random.key(seed), 9)
    part_splits = jax.random.split(jax.random.fold_in(splits[8], part), 9)
    return {
        "queries": draw_queries(jax.random.fold_in(jax.random.fold_in(splits[8], part), 71), part),
        "keys": draw_keys(jax.random.fold_in(jax.random.fold_in(splits[8], part), 71), part),
        "values": centred(part_splits[2], (SEQUENCE_LENGTH, HEAD_COUNT, E), 1.0, 6.0, ((0, 4), (1, 4))),
        "delta_keys": centred(part_splits[3], (SEQUENCE_LENGTH, 2, HEAD_COUNT, E), 1.0, 6.0, ((0, 4), (2, 4))),
        "delta_values": centred(part_splits[4], (SEQUENCE_LENGTH, 2, HEAD_COUNT, E), 1.0, 6.0, ((0, 4), (2, 4))),
        "betas": jnp.clip(0.2 + 1.5999999 * jax.random.uniform(part_splits[5], (2, HEAD_COUNT, SEQUENCE_LENGTH), jnp.float32) ** shard_levels(part_splits[5], (2, HEAD_COUNT, SEQUENCE_LENGTH), ((1, 4), (2, 4)), -0.2, 0.2), 0.2, 1.8),
        "decays": draw_decays(jax.random.fold_in(jax.random.fold_in(splits[8], part), 71), part),
        "grad_out": centred(part_splits[7], (SEQUENCE_LENGTH, HEAD_COUNT, E), 1.0, 6.0, ((0, 4), (1, 4))),
    }


PRECISE = lax.Precision.HIGHEST
EPS = 1e-06

def rounded(array):
    return lax.optimization_barrier(array.astype(jnp.bfloat16)).astype(jnp.float32)

def window_attention(query_rows, key_rows, start):
    block_rows = query_rows.shape[0]
    scores = jnp.einsum('qhe,khe->hqk', query_rows.astype(jnp.float32), key_rows.astype(jnp.float32)) * (1.0 / math.sqrt(E))
    query_pos = start + jnp.arange(block_rows, dtype=jnp.int32)
    key_pos = start - WINDOW + jnp.arange(WINDOW + block_rows, dtype=jnp.int32)
    visible = (key_pos[None, :] <= query_pos[:, None]) & (key_pos[None, :] > query_pos[:, None] - WINDOW) & (key_pos[None, :] >= 0)
    top = lax.optimization_barrier(jnp.max(jnp.where(visible, scores, -jnp.inf), axis=-1, keepdims=True))
    lifted = jnp.where(visible, jnp.exp(jnp.where(visible, scores - top, 0.0)), 0.0)
    total = lax.optimization_barrier(jnp.sum(lifted, axis=-1, keepdims=True))
    return lifted / total

def delta_forward(query, keys_float, values_float, beta, decay):
    query_norm = query / jnp.sqrt(lax.optimization_barrier(jnp.mean(query * query, axis=-1, keepdims=True)) + EPS)
    key_norm = keys_float / jnp.sqrt(lax.optimization_barrier(jnp.sum(keys_float * keys_float, axis=-1, keepdims=True)) + EPS)

    def step(state, inputs):
        query_t, keys_t, values_t, beta_t, decay_t = inputs
        state = decay_t * state
        for mirror in range(2):
            recalled = jnp.dot(keys_t[mirror], state, precision=PRECISE)
            state = state + beta_t[mirror] * jnp.outer(keys_t[mirror], values_t[mirror] - recalled)
        return (state, jnp.dot(query_t, state, precision=PRECISE))
    start = jnp.zeros((E, E), jnp.float32)
    final, outputs = lax.scan(jax.checkpoint(step), start, (query_norm, key_norm, values_float, beta, decay))
    return outputs

def delta_backward(attended, delta_keys, delta_values, betas, decays, grad_out):
    query = rounded(attended).transpose(1, 0, 2)
    keys_float = delta_keys.astype(jnp.float32).transpose(2, 0, 1, 3)
    values_float = delta_values.astype(jnp.float32).transpose(2, 0, 1, 3)
    beta = betas.transpose(1, 2, 0)
    cotangent = grad_out.astype(jnp.float32).transpose(1, 0, 2)

    def per_head(items):
        head_query, head_keys, head_values, head_beta, head_decay, head_cot = items
        pull = jax.vjp(delta_forward, head_query, head_keys, head_values, head_beta, head_decay)[1]
        return pull(head_cot)
    grads = lax.map(per_head, (query, keys_float, values_float, beta, decays, cotangent))
    return (grads[0].transpose(1, 0, 2), grads[1].transpose(1, 2, 0, 3), grads[2].transpose(1, 2, 0, 3), grads[3].transpose(2, 0, 1), grads[4])

def reference(queries, keys, values, delta_keys, delta_values, betas, decays, grad_out):
    block_rows = math.gcd(SEQUENCE_LENGTH, 512)
    count = SEQUENCE_LENGTH // block_rows
    scale = 1.0 / math.sqrt(E)
    padding = jnp.zeros((WINDOW, HEAD_COUNT, E), queries.dtype)
    keys_pad = jnp.concatenate([padding, keys], axis=0)
    values_pad = jnp.concatenate([padding, values], axis=0)

    def slices(start):
        query_rows = lax.dynamic_slice_in_dim(queries, start, block_rows, 0)
        key_rows = lax.dynamic_slice_in_dim(keys_pad, start, WINDOW + block_rows, 0)
        value_rows = lax.dynamic_slice_in_dim(values_pad, start, WINDOW + block_rows, 0)
        return (query_rows, key_rows, value_rows)

    def forward(block):
        start = (block * block_rows).astype(jnp.int32)
        query_rows, key_rows, value_rows = slices(start)
        attention_low = rounded(window_attention(query_rows, key_rows, start))
        return jnp.einsum('hqk,khe->qhe', attention_low, value_rows.astype(jnp.float32))
    mixed = lax.map(forward, jnp.arange(count, dtype=jnp.int32)).reshape(SEQUENCE_LENGTH, HEAD_COUNT, E)
    attended = mixed.astype(jnp.bfloat16)
    grad_attended, grad_dkeys, grad_dvalues, grad_betas, grad_decays = delta_backward(attended, delta_keys, delta_values, betas, decays, grad_out)
    grad_mixed = grad_attended.astype(jnp.bfloat16)

    def backward(carry, block):
        key_acc, value_acc = carry
        start = (block * block_rows).astype(jnp.int32)
        query_rows, key_rows, value_rows = slices(start)
        attention = window_attention(query_rows, key_rows, start)
        attention_low = rounded(attention)
        grad_rows = rounded(lax.dynamic_slice_in_dim(grad_mixed, start, block_rows, 0))
        mixed_rows = lax.dynamic_slice_in_dim(mixed, start, block_rows, 0)
        row_dots = lax.optimization_barrier(jnp.sum(grad_rows * mixed_rows, axis=-1)).T
        grad_attention = jnp.einsum('qhe,khe->hqk', grad_rows, value_rows.astype(jnp.float32))
        grad_scores = rounded(attention * (grad_attention - row_dots[:, :, None]) * scale)
        grad_query_rows = jnp.einsum('hqk,khe->qhe', grad_scores, key_rows.astype(jnp.float32)).astype(jnp.bfloat16)
        key_part = jnp.einsum('hqk,qhe->khe', grad_scores, query_rows.astype(jnp.float32))
        value_part = jnp.einsum('hqk,qhe->khe', attention_low, grad_rows)
        key_acc = lax.dynamic_update_slice_in_dim(key_acc, lax.dynamic_slice_in_dim(key_acc, start, WINDOW + block_rows, 0) + key_part, start, 0)
        value_acc = lax.dynamic_update_slice_in_dim(value_acc, lax.dynamic_slice_in_dim(value_acc, start, WINDOW + block_rows, 0) + value_part, start, 0)
        return ((key_acc, value_acc), grad_query_rows)
    empty = jnp.zeros((WINDOW + SEQUENCE_LENGTH, HEAD_COUNT, E), jnp.float32)
    (key_acc, value_acc), grad_query_blocks = lax.scan(backward, (empty, empty), jnp.arange(count, dtype=jnp.int32))
    grad_queries = grad_query_blocks.reshape(SEQUENCE_LENGTH, HEAD_COUNT, E)
    grad_keys = key_acc[WINDOW:].astype(jnp.bfloat16)
    grad_values = value_acc[WINDOW:].astype(jnp.bfloat16)
    return (grad_queries, grad_keys, grad_values, grad_dkeys.astype(jnp.bfloat16), grad_dvalues.astype(jnp.bfloat16), grad_betas, grad_decays)
```

```python
import functools, math
import jax
import jax.numpy as jnp
from jax import lax
from jax.experimental import pallas as pl
from jax.experimental.pallas import tpu as pltpu
from jax.sharding import PartitionSpec as P

WINDOW = 1024

F32 = jnp.float32
BF16 = jnp.bfloat16
EPS = 1e-06
C = 64
N = 128
LIMIT = 56 * 1024 * 1024


def split(a):
    high = a.astype(BF16)
    return high, (a - high.astype(F32)).astype(BF16)


def contract(a, b, ca, cb):
    return lax.dot_general(a, b, (((ca,), (cb,)), ((), ())), preferred_element_type=F32)


def mm(a, b):
    ah, al = split(a)
    bh, bl = split(b)
    wide = jnp.concatenate([bh, bl], axis=1)
    both = contract(jnp.concatenate([ah, al], axis=1), jnp.concatenate([wide, wide], axis=0), 1, 0)
    half = b.shape[1]
    return both[:, :half] + both[:, half:]


def mm_nt(a, b):
    ah, al = split(a)
    bh, bl = split(b)
    tall = jnp.concatenate([bh, bl], axis=0)
    both = contract(jnp.concatenate([ah, al], axis=1), jnp.concatenate([tall, tall], axis=1), 1, 1)
    half = b.shape[0]
    return both[:, :half] + both[:, half:]


def mm_tn(a, b):
    ah, al = split(a)
    bh, bl = split(b)
    wide = jnp.concatenate([bh, bl], axis=1)
    both = contract(jnp.concatenate([ah, al], axis=0), jnp.concatenate([wide, wide], axis=0), 0, 0)
    half = b.shape[1]
    return both[:, :half] + both[:, half:]


def low_nt(low, b):
    bh, bl = split(b)
    both = contract(low, jnp.concatenate([bh, bl], axis=0), 1, 1)
    half = b.shape[0]
    return both[:, :half] + both[:, half:]


def low_tn(a, low):
    ah, al = split(a)
    return contract(jnp.concatenate([ah, al], axis=0), jnp.concatenate([low, low], axis=0), 0, 0)


def iota(shape, axis):
    return lax.broadcasted_iota(jnp.int32, shape, axis)


class Grid:
    def __init__(self):
        self.row = iota((N, N), 0)
        self.lane = iota((N, N), 1)
        self.row_pos = self.row & (C - 1)
        self.lane_pos = self.lane & (C - 1)
        key_row = 2 * self.row_pos + (self.row >> 6)
        key_lane = 2 * self.lane_pos + (self.lane >> 6)
        self.strict = key_row > key_lane
        self.differ = key_row ^ key_lane
        self.diag = self.row == self.lane

    def to_row(self, column):
        return jnp.sum(jnp.where(self.diag, column, 0.0), axis=0, keepdims=True)

    def to_column(self, line):
        return jnp.sum(jnp.where(self.diag, line, 0.0), axis=1, keepdims=True)


def pick_row(block, h):
    return jnp.sum(jnp.where(iota(block.shape, 0) == h, block, 0.0), axis=0, keepdims=True)


def put_row(block, h, line):
    return jnp.where(iota(block.shape, 0) == h, line, block)


def gates(grid, betas_ref, decays_ref, h, c):
    pair, half = c // 2, C * (c % 2)
    lanes = pl.ds(pair * N, N)
    first = pick_row(betas_ref[0, :, lanes], h)
    second = pick_row(betas_ref[1, :, lanes], h)
    logs = jnp.log(pick_row(decays_ref[:, lanes], h))
    offset = grid.lane - half
    chosen = jnp.where(grid.row < C, first, second)
    beta = jnp.sum(jnp.where(offset == grid.row_pos, chosen, 0.0), axis=1, keepdims=True)
    seen = (offset >= 0) & (offset <= grid.row_pos)
    run = jnp.sum(jnp.where(seen, logs, 0.0), axis=1, keepdims=True)
    inside = (offset[:1] >= 0) & (offset[:1] < C)
    end = jnp.sum(jnp.where(inside, logs, 0.0), axis=1, keepdims=True)
    return beta, run, grid.to_row(run), end


def strict_fade(grid, run, line):
    return jnp.where(grid.strict, jnp.exp(jnp.minimum(run - line, 0.0)), 0.0)


def query_fade(grid, run, line):
    seen = grid.lane_pos[:C] <= grid.row_pos[:C]
    return jnp.where(seen, jnp.exp(jnp.minimum(run[:C] - line, 0.0)), 0.0)


def pair_rows(ref, heads, h, c):
    base = c * C * 2 * heads
    return jnp.concatenate(
        [
            ref[pl.ds(base + h, C, stride=2 * heads), :],
            ref[pl.ds(base + heads + h, C, stride=2 * heads), :],
        ],
        axis=0,
    )


def local_kernel(heads, count, dk_ref, dv_ref, betas_ref, decays_ref,
                 k_ref, inv_ref, p_ref, y_ref, t_ref, o_ref, aux_ref, tsh_ref, osh_ref,
                 keys_scr, values_scr):
    h = pl.program_id(0)

    @pl.when(h == 0)
    def _():
        keys_scr[...] = dk_ref[...].astype(F32)
        values_scr[...] = dv_ref[...].astype(F32)

    grid = Grid()
    eye = jnp.where(grid.diag, 1.0, 0.0)
    state = []
    for c in range(count):
        raw = pair_rows(keys_scr, heads, h, c)
        values = pair_rows(values_scr, heads, h, c)
        scale = lax.rsqrt(jnp.sum(raw * raw, axis=1, keepdims=True) + EPS)
        keys = raw * scale
        beta, run, line, end = gates(grid, betas_ref, decays_ref, h, c)
        k_ref[0, c] = keys
        aux_ref[0, c] = jnp.broadcast_to(grid.to_row(scale), (8, N))
        system = beta * strict_fade(grid, run, line) * mm_nt(keys, keys)
        inverse = eye - jnp.where(grid.differ == 1, system, 0.0)
        rhs = jnp.concatenate([(beta * jnp.exp(run)) * keys, beta * values], axis=1)
        state.append([system, inverse, rhs, keys * jnp.exp(end - run), end])
    for level in range(1, 7):
        near = (grid.differ >= (1 << level)) & (grid.differ < (2 << level))
        for item in state:
            item.append(mm(jnp.where(near, item[0], 0.0), item[1]))
        for item in state:
            item[1] = item[1] - mm(item[1], item.pop())
    for c, item in enumerate(state):
        inv_ref[0, c] = item[1]
        both = mm(item[1], item[2])
        p_ref[0, c] = both[:, :N]
        y_ref[0, c] = both[:, N:]
        maps = mm_tn(item[3], both)
        item.append(jnp.concatenate([jnp.exp(item[4]) * eye - maps[:, :N], maps[:, N:]], axis=1))
        t_ref[0, c] = item[5][:, :N]
        o_ref[0, c] = item[5][:, N:]
    total = state[0][5]
    zero = jnp.zeros((N, N), F32)
    for c in range(1, count):
        step = state[c][5]
        total = mm(step[:, :N], total) + jnp.concatenate([zero, step[:, N:]], axis=1)
    tsh_ref[0] = total[:, :N]
    osh_ref[0] = total[:, N:]


def place_index(place, s, total):
    return lax.rem(place + s, total)


def readout_kernel(heads, count, place_ref, g_ref, betas_ref, decays_ref, s_in_ref,
                   k_ref, p_ref, y_ref, t_ref, o_ref,
                   s_ref, u_ref, dw_ref, dq_ref, *rest):
    outs, (g_scr, dq_scr, sem) = rest[:heads], rest[heads:]
    h = pl.program_id(0)

    @pl.when(h == 0)
    def _():
        g_scr[...] = g_ref[...].astype(F32)

    grid = Grid()
    current = s_in_ref[0].astype(F32)
    s_ref[0, 0] = current
    updates = []
    states = [current]
    for c in range(count):
        both = mm(jnp.concatenate([t_ref[0, c], p_ref[0, c]], axis=0), current)
        updates.append(y_ref[0, c] - both[N:])
        current = both[:N] + o_ref[0, c]
        u_ref[0, c] = updates[c]
        s_ref[0, c + 1] = current
        states.append(current)
    for c in range(count):
        beta, run, line, end = gates(grid, betas_ref, decays_ref, h, c)
        cot = g_scr[pl.ds(c * C * heads + h, C, stride=heads), :].astype(BF16)
        both = low_nt(cot, jnp.concatenate([updates[c], states[c]], axis=0))
        weights = both[:, :N] * query_fade(grid, run, line)
        dw_ref[0, c] = weights
        grad = mm(weights, k_ref[0, c]) + jnp.exp(run[:C]) * both[:, N:]
        dq_ref[0, c] = grad
        dq_scr[h, pl.ds(c * C, C), :] = grad.astype(BF16)

    @pl.when(h == heads - 1)
    def _():
        copies = []
        for s in range(heads):
            target = place_index(place_ref[0], s, heads)
            copies.append(pltpu.make_async_copy(dq_scr.at[target], outs[s], sem.at[s]))
        for copy in copies:
            copy.start()
        for copy in copies:
            copy.wait()


def unit_queries(low):
    raw = low.astype(F32)
    return raw * lax.rsqrt(jnp.mean(raw * raw, axis=1, keepdims=True) + EPS)


def source_kernel(heads, count, place_ref, g_ref, betas_ref, decays_ref, k_ref, p_ref, t_ref, *rest):
    ins, (q_ref, z_ref, b_ref, bsh_ref, g_scr, q_scr, sem) = rest[:heads], rest[heads:]
    h = pl.program_id(0)

    @pl.when(h == 0)
    def _():
        copies = []
        for s in range(heads):
            target = lax.rem(place_ref[0] + heads - s, heads)
            copies.append(pltpu.make_async_copy(ins[s], q_scr.at[target], sem.at[s]))
        for copy in copies:
            copy.start()
        g_scr[...] = g_ref[...].astype(F32)
        for copy in copies:
            copy.wait()

    grid = Grid()
    sources = []
    for c in range(count):
        beta, run, line, end = gates(grid, betas_ref, decays_ref, h, c)
        query = unit_queries(q_scr[h, pl.ds(c * C, C), :])
        q_ref[0, c] = query
        cot = g_scr[pl.ds(c * C * heads + h, C, stride=heads), :].astype(BF16)
        weights = mm_nt(query, k_ref[0, c]) * query_fade(grid, run, line)
        z = low_tn(weights, cot)
        z_ref[0, c] = z
        source = low_tn(query * jnp.exp(run[:C]), cot) - mm_tn(p_ref[0, c], z)
        b_ref[0, c] = source
        sources.append(source)
    total = sources[count - 1]
    for c in range(count - 2, -1, -1):
        total = sources[c] + mm_tn(t_ref[0, c], total)
    bsh_ref[0] = total


def final_kernel(heads, count, betas_ref, decays_ref, lam_ref, k_ref, inv_ref, t_ref, aux_ref,
                 s_ref, u_ref, dw_ref, dq_ref, q_ref, z_ref, b_ref,
                 gk_ref, gv_ref, gb_ref, gd_ref, gk_scr, gv_scr):
    h = pl.program_id(0)
    grid = Grid()
    lam = [None] * count
    lam[count - 1] = lam_ref[0].astype(F32)
    for c in range(count - 1, 0, -1):
        lam[c - 1] = mm_tn(t_ref[0, c], lam[c]) + b_ref[0, c]
    lines = [[], [], []]
    for c in range(count):
        beta, run, line, end = gates(grid, betas_ref, decays_ref, h, c)
        keys, upd, inverse, state, later = k_ref[0, c], u_ref[0, c], inv_ref[0, c], s_ref[0, c], lam[c]
        tail = jnp.exp(end - run)
        du = z_ref[0, c] + mm(keys * tail, later)
        r = mm_tn(inverse, du)
        gb = jnp.sum(r * upd, axis=1, keepdims=True) / beta
        both = mm_nt(r, jnp.concatenate([upd, state], axis=0))
        d = -both[:, :N] * (beta * strict_fade(grid, run, line))
        read = mm(d, keys) - (beta * jnp.exp(run)) * both[:, N:]
        query = q_ref[0, c]
        write = mm_tn(d, keys) + tail * mm_nt(upd, later) + mm_tn(dw_ref[0, c], query)
        grad = read + write
        scale = grid.to_column(aux_ref[0, c][:1])
        gk = scale * (grad - keys * jnp.sum(keys * grad, axis=1, keepdims=True))
        gv = beta * r
        base = c * C * 2 * heads
        for m in range(2):
            rows = pl.ds(base + m * heads + h, C, stride=2 * heads)
            gk_scr[rows, :] = gk[m * C:(m + 1) * C]
            gv_scr[rows, :] = gv[m * C:(m + 1) * C]
        pulls = jnp.sum(keys * (read - write), axis=1, keepdims=True)
        asks = jnp.sum(query * dq_ref[0, c], axis=1, keepdims=True)
        pulls = pulls[:C] + pulls[C:] + asks
        after = grid.row_pos[:C] >= grid.lane_pos[:C]
        total = jnp.sum(jnp.sum(s_ref[0, c + 1] * later, axis=1, keepdims=True), axis=0, keepdims=True)
        gd = jnp.sum(jnp.where(after, pulls, 0.0), axis=0, keepdims=True) + total
        half = C * (c % 2)
        mine = (grid.lane[:1] >= half) & (grid.lane[:1] < half + C)
        lines[2].append(jnp.where(mine, gd, 0.0))
        for m in range(2):
            pick = (grid.lane - half == grid.row - m * C) & (grid.row >= m * C) & (grid.row < (m + 1) * C)
            lines[m].append(jnp.sum(jnp.where(pick, gb, 0.0), axis=0, keepdims=True))
    for p in range(count // 2):
        lanes = pl.ds(p * N, N)
        for m in range(2):
            gb_ref[m, :, lanes] = put_row(gb_ref[m, :, lanes], h, lines[m][2 * p] + lines[m][2 * p + 1])
        gd = (lines[2][2 * p] + lines[2][2 * p + 1]) / decays_ref[:, lanes]
        gd_ref[:, lanes] = put_row(gd_ref[:, lanes], h, gd)

    @pl.when(h == heads - 1)
    def _():
        gk_ref[...] = gk_scr[...].astype(BF16)
        gv_ref[...] = gv_scr[...].astype(BF16)


def full(shape):
    return pl.BlockSpec(shape, lambda h: (0,) * len(shape))


def per_head(shape):
    return pl.BlockSpec((1,) + shape, lambda h: (h,) + (0,) * len(shape))


ANY = pl.BlockSpec(memory_space=pl.ANY)
SCALAR = pl.BlockSpec(memory_space=pltpu.SMEM)


def shaped(shape, dtype=F32):
    return jax.ShapeDtypeStruct(shape, dtype)


def call(body, name, heads, in_specs, outs, out_specs, scratch, flops):
    return pl.pallas_call(
        body,
        name=name,
        grid=(heads,),
        in_specs=in_specs,
        out_shape=outs,
        out_specs=out_specs,
        scratch_shapes=scratch,
        compiler_params=pltpu.CompilerParams(
            dimension_semantics=("arbitrary",), vmem_limit_bytes=LIMIT
        ),
        cost_estimate=pl.CostEstimate(flops=flops, bytes_accessed=8 << 20, transcendentals=0),
    )


def delta_local(dk, dv, betas, decays):
    heads, rows = decays.shape
    count = rows // C
    big, gate, dec = full(dk.shape), full(betas.shape), full(decays.shape)
    block = per_head((count, N, N))
    square = shaped((heads, count, N, N))
    return call(
        functools.partial(local_kernel, heads, count), "delta_local", heads,
        [big, big, gate, dec],
        [square] * 6 + [shaped((heads, count, 8, N))] + [shaped((heads, N, N))] * 2,
        [block] * 6 + [per_head((count, 8, N))] + [per_head((N, N))] * 2,
        [pltpu.VMEM(dk.shape, F32)] * 2,
        10 << 30,
    )(dk, dv, betas, decays)


def delta_readout(place, g, betas, decays, entry, k, p, y, t, o):
    heads, rows = decays.shape
    count = rows // C
    block, square = per_head((count, N, N)), shaped((heads, count, N, N))
    thin = per_head((count, C, N))
    return call(
        functools.partial(readout_kernel, heads, count), "delta_readout", heads,
        [SCALAR, full(g.shape), full(betas.shape), full(decays.shape), per_head((N, N))] + [block] * 5,
        [shaped((heads, count + 1, N, N)), square] + [shaped((heads, count, C, N))] * 2
        + [shaped((rows, N), BF16)] * heads,
        [per_head((count + 1, N, N)), block, thin, thin] + [ANY] * heads,
        [pltpu.VMEM(g.shape, F32), pltpu.VMEM((heads, rows, N), BF16), pltpu.SemaphoreType.DMA((heads,))],
        3 << 30,
    )(place, g, betas, decays, entry, k, p, y, t, o)


def delta_source(place, g, betas, decays, k, p, t, attended):
    heads, rows = decays.shape
    count = rows // C
    block, square = per_head((count, N, N)), shaped((heads, count, N, N))
    return call(
        functools.partial(source_kernel, heads, count), "delta_source", heads,
        [SCALAR, full(g.shape), full(betas.shape), full(decays.shape)] + [block] * 3 + [ANY] * heads,
        [shaped((heads, count, C, N)), square, square, shaped((heads, N, N))],
        [per_head((count, C, N)), block, block, per_head((N, N))],
        [pltpu.VMEM(g.shape, F32), pltpu.VMEM((heads, rows, N), BF16), pltpu.SemaphoreType.DMA((heads,))],
        3 << 30,
    )(place, g, betas, decays, k, p, t, *attended)


def delta_final(betas, decays, lam, k, inv, t, aux, s, u, dw, dq, q, z, b):
    heads, rows = decays.shape
    count = rows // C
    block = per_head((count, N, N))
    thin = per_head((count, C, N))
    wide = (2 * rows * heads, N)
    return call(
        functools.partial(final_kernel, heads, count), "delta_final", heads,
        [full(betas.shape), full(decays.shape), per_head((N, N)), block, block, block,
         per_head((count, 8, N)), per_head((count + 1, N, N)), block, thin, thin, thin, block, block],
        [shaped(wide, BF16), shaped(wide, BF16), shaped(betas.shape), shaped(decays.shape)],
        [full(wide), full(wide), full(betas.shape), full(decays.shape)],
        [pltpu.VMEM(wide, F32)] * 2,
        8 << 30,
    )(betas, decays, lam, k, inv, t, aux, s, u, dw, dq, q, z, b)


def rounds(refs, index, count, sign):
    return [lax.rem(index + (s if sign > 0 else count - s), count) for s in range(count)]


def send_kernel(count, place_ref, q_ref, k_ref, v_ref, *rest):
    outs, (scr,) = rest[:count], rest[count:]
    heads = count
    rows = q_ref.shape[0] // heads
    for m, ref in enumerate((q_ref, k_ref, v_ref)):
        scr[...] = ref[...].astype(F32)
        for s in range(count):
            head = lax.rem(place_ref[0] + s, count)
            outs[s][m] = scr[pl.ds(head, rows, stride=heads), :].astype(BF16)


def take_kernel(count, place_ref, *rest):
    ins, outs, (scr,) = rest[:count], rest[count:count + 3], rest[count + 3:]
    heads = count
    rows = outs[0].shape[0] // heads
    for m in range(3):
        for s in range(count):
            head = lax.rem(place_ref[0] + count - s, count)
            scr[pl.ds(head, rows, stride=heads), :] = ins[s][m].astype(F32)
        outs[m][...] = scr[...].astype(BF16)


def gather_blocks(place_ref, refs, scr, sem, first):
    copies = []
    count = len(refs)
    for s in range(count):
        source = lax.rem(place_ref[0] + count - s, count)
        copies.append(pltpu.make_async_copy(refs[s], scr.at[source], sem.at[first + s]))
    return copies


def scatter_blocks(place_ref, scr, refs, sem, first):
    copies = []
    count = len(refs)
    for s in range(count):
        target = lax.rem(place_ref[0] + s, count)
        copies.append(pltpu.make_async_copy(scr.at[target], refs[s], sem.at[first + s]))
    return copies


def attend_kernel(count, scale, place_ref, *rest):
    ins, (prob_ref, mixed_ref), outs = rest[:count], rest[count:count + 2], rest[count + 2:2 * count + 2]
    scr, att_scr, sem = rest[2 * count + 2:]
    copies = gather_blocks(place_ref, ins, scr, sem, 0)
    for copy in copies:
        copy.start()
    for copy in copies:
        copy.wait()
    rows = scr.shape[2]
    causal = iota((rows, rows), 0) <= iota((rows, rows), 1)
    for i in range(count):
        query = scr[i, 0]
        pieces = []
        for j in range(i + 1):
            score = contract(scr[j, 1], query, 1, 1) * scale
            pieces.append(jnp.where(causal, score, -jnp.inf) if j == i else score)
        top = pieces[0].max(axis=0, keepdims=True)
        for piece in pieces[1:]:
            top = jnp.maximum(top, piece.max(axis=0, keepdims=True))
        pieces = [jnp.exp(piece - top) for piece in pieces]
        total = pieces[0].sum(axis=0, keepdims=True)
        for piece in pieces[1:]:
            total = total + piece.sum(axis=0, keepdims=True)
        mixed = None
        for j, piece in enumerate(pieces):
            low = (piece / total).astype(BF16)
            prob_ref[i * (i + 1) // 2 + j] = low
            term = contract(low, scr[j, 2], 0, 0)
            mixed = term if mixed is None else mixed + term
        mixed_ref[i] = mixed
        att_scr[i] = mixed.astype(BF16)
    copies = scatter_blocks(place_ref, att_scr, outs, sem, 0)
    for copy in copies:
        copy.start()
    for copy in copies:
        copy.wait()


def attend_back_kernel(count, scale, place_ref, prob_ref, mixed_ref, *rest):
    ins, grads, outs = rest[:count], rest[count:2 * count], rest[2 * count:3 * count]
    scr, g_scr, out_scr, acc, sem = rest[3 * count:]
    copies = gather_blocks(place_ref, ins, scr, sem, 0) + gather_blocks(place_ref, grads, g_scr, sem, count)
    for copy in copies:
        copy.start()
    for copy in copies:
        copy.wait()
    rows = scr.shape[2]
    ones = jnp.ones((8, N), F32)
    for i in range(count):
        mixed = mixed_ref[i]
        low = mixed.astype(BF16).astype(F32)
        grad = g_scr[i].astype(F32)
        inv = lax.rsqrt(jnp.mean(low * low, axis=1, keepdims=True) + EPS)
        pull = inv * (grad - low * (inv * inv * jnp.mean(low * grad, axis=1, keepdims=True)))
        pull = pull.astype(BF16)
        dots = mm_nt(ones, pull.astype(F32) * mixed)[:1]
        query = scr[i, 0]
        gq = None
        for j in range(i + 1):
            prob = prob_ref[i * (i + 1) // 2 + j]
            gp = contract(scr[j, 2], pull, 1, 1)
            gs = (prob.astype(F32) * (gp - dots) * scale).astype(BF16)
            term = contract(gs, scr[j, 1], 0, 0)
            gq = term if gq is None else gq + term
            gk = contract(gs, query, 1, 0)
            gv = contract(prob, pull, 1, 0)
            if i == j:
                acc[j, 0] = gk
                acc[j, 1] = gv
            else:
                acc[j, 0] = acc[j, 0] + gk
                acc[j, 1] = acc[j, 1] + gv
        out_scr[i, 0] = gq.astype(BF16)
    for j in range(count):
        out_scr[j, 1] = acc[j, 0].astype(BF16)
        out_scr[j, 2] = acc[j, 1].astype(BF16)
    copies = scatter_blocks(place_ref, out_scr, outs, sem, 0)
    for copy in copies:
        copy.start()
    for copy in copies:
        copy.wait()


VM = pl.BlockSpec(memory_space=pltpu.VMEM)


def single(body, name, in_specs, outs, out_specs, scratch, flops):
    return pl.pallas_call(
        body,
        name=name,
        in_specs=in_specs,
        out_shape=outs,
        out_specs=out_specs,
        scratch_shapes=scratch,
        compiler_params=pltpu.CompilerParams(vmem_limit_bytes=LIMIT),
        cost_estimate=pl.CostEstimate(flops=flops, bytes_accessed=4 << 20, transcendentals=0),
    )


def send_heads(place, q, k, v, count):
    rows = q.shape[0] // count
    return single(
        functools.partial(send_kernel, count), "send_heads",
        [SCALAR, VM, VM, VM], [shaped((3, rows, N), BF16)] * count, [VM] * count,
        [pltpu.VMEM(q.shape, F32)], 1 << 28,
    )(place, q, k, v)


def take_heads(place, parts):
    count = len(parts)
    rows = parts[0].shape[1]
    wide = (rows * count, N)
    return single(
        functools.partial(take_kernel, count), "take_heads",
        [SCALAR] + [VM] * count, [shaped(wide, BF16)] * 3, [VM] * 3,
        [pltpu.VMEM(wide, F32)], 1 << 28,
    )(place, *parts)


def attend(place, parts, scale):
    count = len(parts)
    rows = parts[0].shape[1]
    tri = count * (count + 1) // 2
    return single(
        functools.partial(attend_kernel, count, scale), "attend",
        [SCALAR] + [ANY] * count,
        [shaped((tri, rows, rows), BF16), shaped((count, rows, N))] + [shaped((rows, N), BF16)] * count,
        [VM, VM] + [ANY] * count,
        [pltpu.VMEM((count, 3, rows, N), BF16), pltpu.VMEM((count, rows, N), BF16),
         pltpu.SemaphoreType.DMA((count,))], 2 << 30,
    )(place, *parts)


def attend_back(place, prob, mixed, parts, grads, scale):
    count = len(parts)
    rows = parts[0].shape[1]
    return single(
        functools.partial(attend_back_kernel, count, scale), "attend_back",
        [SCALAR, VM, VM] + [ANY] * (2 * count),
        [shaped((3, rows, N), BF16)] * count, [ANY] * count,
        [pltpu.VMEM((count, 3, rows, N), BF16), pltpu.VMEM((count, rows, N), BF16),
         pltpu.VMEM((count, 3, rows, N), BF16), pltpu.VMEM((count, 2, rows, N), F32),
         pltpu.SemaphoreType.DMA((2 * count,))], 4 << 30,
    )(place, prob, mixed, *parts, *grads)


PRECISE = lax.Precision.HIGHEST


def shifted(value, axis, steps):
    count = lax.axis_size(axis)
    initial, last = (max(0, -steps), min(count, count - steps))
    return lax.ppermute(value, axis, [(source, source + steps) for source in range(initial, last)])


def rotated(parts, axis):
    count = len(parts)
    moved = [parts[0]]
    for s in range(1, count):
        moved.append(lax.ppermute(parts[s], axis, [(d, (d + s) % count) for d in range(count)]))
    return moved


def apply_map(matrix, state):
    return jnp.einsum("hij,hjk->hik", matrix, state, precision=PRECISE)


def entering(matrix, offset, axis, step):
    count = lax.axis_size(axis)
    if count <= 4:
        state = shifted(offset.astype(BF16), axis, step)
        for hop in range(count - 2):
            state = shifted((apply_map(matrix, state.astype(F32)) + offset).astype(BF16), axis, step)
        return state
    place = lax.axis_index(axis)
    place = place if step > 0 else count - 1 - place
    eye = jnp.eye(matrix.shape[-1], dtype=F32)
    reach = 1
    while reach < count:
        before, start = (shifted(matrix, axis, step * reach), shifted(offset, axis, step * reach))
        before = before + jnp.where(place < reach, eye, 0.0)
        offset = apply_map(matrix, start) + offset
        matrix = apply_map(matrix, before)
        reach *= 2
    return shifted(offset, axis, step).astype(BF16)


def visible_pairs(rows, span):
    relative = jnp.arange((span + 1) * rows, dtype=jnp.int32) - span * rows
    local = jnp.arange(rows, dtype=jnp.int32)
    return (
        (relative[None, :] <= local[:, None])
        & (relative[None, :] > local[:, None] - WINDOW)
        & (lax.axis_index("seq") * rows + relative[None, :] >= 0)
    )


def window_forward(queries, keys, values, scale):
    rows = queries.shape[0]
    span = -(-WINDOW // rows)
    couple = jnp.stack([keys, values])
    earlier = [shifted(couple, "seq", step + 1) for step in range(min(span, lax.axis_size("seq") - 1))]
    span = len(earlier)
    ordered = earlier[::-1] + [couple]
    window_keys = jnp.concatenate([piece[0] for piece in ordered], axis=0)
    window_values = jnp.concatenate([piece[1] for piece in ordered], axis=0)
    visible = visible_pairs(rows, span)
    scores = jnp.einsum("qhe,khe->hqk", queries, window_keys, preferred_element_type=F32) * scale
    top = jnp.max(jnp.where(visible, scores, -jnp.inf), axis=-1)
    lifted = jnp.where(visible, jnp.exp(jnp.where(visible, scores - top[:, :, None], 0.0)), 0.0)
    attention = lifted / jnp.sum(lifted, axis=-1)[:, :, None]
    mixed = jnp.einsum(
        "hqk,khe->qhe", attention.astype(BF16), window_values, preferred_element_type=F32
    )
    return window_keys, window_values, attention, mixed, span


def window_backward(queries, window_keys, window_values, attention, mixed, span, unit_grad, scale):
    rows = queries.shape[0]
    low = mixed.astype(BF16).astype(F32)
    grad = unit_grad.astype(F32)
    inv = lax.rsqrt(jnp.mean(low * low, axis=-1, keepdims=True) + EPS)
    pull = inv * (grad - low * (inv * inv * jnp.mean(low * grad, axis=-1, keepdims=True)))
    pull = pull.astype(BF16)
    row_dots = jnp.sum(pull.astype(F32) * mixed, axis=-1).T
    grad_attention = jnp.einsum("qhe,khe->hqk", pull, window_values, preferred_element_type=F32)
    grad_scores = (attention * (grad_attention - row_dots[:, :, None]) * scale).astype(BF16)
    grad_queries = jnp.einsum(
        "hqk,khe->qhe", grad_scores, window_keys, preferred_element_type=F32
    ).astype(BF16)
    key_parts = jnp.einsum("hqk,qhe->khe", grad_scores, queries, preferred_element_type=F32)
    value_parts = jnp.einsum("hqk,qhe->khe", attention.astype(BF16), pull, preferred_element_type=F32)
    gathered = jnp.stack([key_parts[span * rows:], value_parts[span * rows:]])
    for later in range(1, span + 1):
        first = (span - later) * rows
        piece = jnp.stack([key_parts[first:first + rows], value_parts[first:first + rows]])
        gathered = gathered + shifted(piece, "seq", -later)
    return grad_queries, gathered[0].astype(BF16), gathered[1].astype(BF16)


def body(queries, keys, values, delta_keys, delta_values, betas, decays, grad_out):
    rows, heads, width = queries.shape
    scale = 1.0 / math.sqrt(width)
    count = lax.axis_size("seq")
    by_head = heads == count and WINDOW >= count * rows

    def flat(array):
        return array.reshape(-1, width)

    place = lax.axis_index("seq").astype(jnp.int32).reshape(1) if by_head else jnp.zeros((1,), jnp.int32)
    if by_head:
        parts = rotated(send_heads(place, flat(queries), flat(keys), flat(values), count), "seq")
    cot = flat(grad_out)
    k, inverse, p, y, t, o, aux, shard_map, shard_offset = delta_local(
        flat(delta_keys), flat(delta_values), betas, decays
    )
    entry = entering(shard_map, shard_offset, "seq", 1)
    if by_head:
        prob, mixed, *attended = attend(place, parts, scale)
        attended = rotated(attended, "seq")
    else:
        saved = window_forward(queries, keys, values, scale)
        low = saved[3].astype(BF16)
        attended = [low[:, (heads - s) % heads] for s in range(heads)]
    s, u, dw, dq, *pulls = delta_readout(place, cot, betas, decays, entry, k, p, y, t, o)
    if by_head:
        pulls = rotated(pulls, "seq")
        outs = rotated(attend_back(place, prob, mixed, parts, pulls, scale), "seq")
        grads = [array.reshape(rows, heads, width) for array in take_heads(place, outs)]
    else:
        grads = window_backward(queries, *saved, jnp.stack(pulls, axis=1), scale)
    q, z, b, shard_source = delta_source(place, cot, betas, decays, k, p, t, attended)
    leaving = entering(jnp.swapaxes(shard_map, 1, 2), shard_source, "seq", -1)
    grad_keys, grad_values, grad_betas, grad_decays = delta_final(
        betas, decays, leaving, k, inverse, t, aux, s, u, dw, dq, q, z, b
    )
    pair = (rows, 2, heads, width)
    return (*grads, grad_keys.reshape(pair), grad_values.reshape(pair), grad_betas, grad_decays)


def solution(mesh):
    row = P(("parts", "seq"), "head", None)
    pair = P(("parts", "seq"), None, "head", None)
    beta = P(None, "head", ("parts", "seq"))
    decay = P("head", ("parts", "seq"))
    return jax.shard_map(
        body,
        mesh=mesh,
        in_specs=(row, row, row, pair, pair, beta, decay, row),
        out_specs=(row, row, row, pair, pair, beta, decay),
        check_vma=False,
    )
```

```python
import functools, math
import jax
import jax.numpy as jnp
from jax import lax
from jax.experimental import pallas as pl
from jax.experimental.pallas import tpu as pltpu
from jax.sharding import PartitionSpec as P

WINDOW = 1024

F32 = jnp.float32
BF16 = jnp.bfloat16
EPS = 1e-06
C = 64
N = 128
LIMIT = 16 * 1024 * 1024


def split(a):
    high = a.astype(BF16)
    return high, (a - high.astype(F32)).astype(BF16)


def contract(a, b, ca, cb):
    return lax.dot_general(a, b, (((ca,), (cb,)), ((), ())), preferred_element_type=F32)


def mm(a, b):
    ah, al = split(a)
    bh, bl = split(b)
    wide = jnp.concatenate([bh, bl], axis=1)
    both = contract(jnp.concatenate([ah, al], axis=1), jnp.concatenate([wide, wide], axis=0), 1, 0)
    half = b.shape[1]
    return both[:, :half] + both[:, half:]


def mm_nt(a, b):
    ah, al = split(a)
    bh, bl = split(b)
    tall = jnp.concatenate([bh, bl], axis=0)
    both = contract(jnp.concatenate([ah, al], axis=1), jnp.concatenate([tall, tall], axis=1), 1, 1)
    half = b.shape[0]
    return both[:, :half] + both[:, half:]


def mm_tn(a, b):
    ah, al = split(a)
    bh, bl = split(b)
    wide = jnp.concatenate([bh, bl], axis=1)
    both = contract(jnp.concatenate([ah, al], axis=0), jnp.concatenate([wide, wide], axis=0), 0, 0)
    half = b.shape[1]
    return both[:, :half] + both[:, half:]


def low_nt(low, b):
    bh, bl = split(b)
    both = contract(low, jnp.concatenate([bh, bl], axis=0), 1, 1)
    half = b.shape[0]
    return both[:, :half] + both[:, half:]


def low_tn(a, low):
    ah, al = split(a)
    return contract(jnp.concatenate([ah, al], axis=0), jnp.concatenate([low, low], axis=0), 0, 0)


def iota(shape, axis):
    return lax.broadcasted_iota(jnp.int32, shape, axis)


class Grid:
    def __init__(self):
        self.row = iota((N, N), 0)
        self.lane = iota((N, N), 1)
        self.row_pos = self.row & (C - 1)
        self.lane_pos = self.lane & (C - 1)
        key_row = 2 * self.row_pos + (self.row >> 6)
        key_lane = 2 * self.lane_pos + (self.lane >> 6)
        self.strict = key_row > key_lane
        self.differ = key_row ^ key_lane
        self.diag = self.row == self.lane

    def to_row(self, column):
        return jnp.sum(jnp.where(self.diag, column, 0.0), axis=0, keepdims=True)

    def to_column(self, line):
        return jnp.sum(jnp.where(self.diag, line, 0.0), axis=1, keepdims=True)


def gates(grid, betas_ref, decays_ref, h, c):
    pair, half = c // 2, C * (c % 2)
    lanes = pl.ds(pair * N, N)
    first = betas_ref[0, pl.ds(h, 1), lanes]
    second = betas_ref[1, pl.ds(h, 1), lanes]
    logs = jnp.log(decays_ref[pl.ds(h, 1), lanes])
    offset = grid.lane - half
    chosen = jnp.where(grid.row < C, first, second)
    beta = jnp.sum(jnp.where(offset == grid.row_pos, chosen, 0.0), axis=1, keepdims=True)
    seen = (offset >= 0) & (offset <= grid.row_pos)
    run = jnp.sum(jnp.where(seen, logs, 0.0), axis=1, keepdims=True)
    inside = (offset[:1] >= 0) & (offset[:1] < C)
    end = jnp.sum(jnp.where(inside, logs, 0.0), axis=1, keepdims=True)
    return beta, run, grid.to_row(run), end


def pair_rows(ref, heads, h, c):
    base = c * C * 2 * heads
    return jnp.concatenate(
        [
            ref[pl.ds(base + h, C, stride=2 * heads), :],
            ref[pl.ds(base + heads + h, C, stride=2 * heads), :],
        ],
        axis=0,
    )


BETA, READ, TAIL, SCALE = range(4)


def local_kernel(heads, count, dk_ref, dv_ref, betas_ref, decays_ref,
                 k_ref, kt_ref, inv_ref, p_ref, y_ref, t_ref, o_ref, fade_ref, see_ref, run_ref, col_ref,
                 tsh_ref, osh_ref, low_scr, keys_scr, values_scr, sys_scr, rhs_scr, sem):
    copies = [pltpu.make_async_copy(ref, low_scr.at[m], sem.at[m]) for m, ref in enumerate((dk_ref, dv_ref))]
    for copy in copies:
        copy.start()
    grid = Grid()
    for m, scr in enumerate((keys_scr, values_scr)):
        copies[m].wait()
        scr[...] = low_scr[m].astype(F32)
    eye = jnp.where(grid.diag, 1.0, 0.0)
    items = [(h, c) for h in range(heads) for c in range(count)]
    ends = {}
    for h, c in items:
        raw = pair_rows(keys_scr, heads, h, c)
        values = pair_rows(values_scr, heads, h, c)
        scale = lax.rsqrt(jnp.sum(raw * raw, axis=1, keepdims=True) + EPS)
        keys = raw * scale
        beta, run, line, end = gates(grid, betas_ref, decays_ref, h, c)
        tail = jnp.exp(end - run)
        read = beta * jnp.exp(run)
        fade = beta * jnp.where(grid.strict, jnp.exp(jnp.minimum(run - line, 0.0)), 0.0)
        seen = grid.lane_pos[:C] <= grid.row_pos[:C]
        see_ref[h, c] = jnp.where(seen, jnp.exp(jnp.minimum(run[:C] - line, 0.0)), 0.0)
        run_ref[h, c] = jnp.broadcast_to(jnp.exp(run[:C]), (C, N))
        col_ref[h, c] = jnp.where(
            grid.lane == BETA, beta,
            jnp.where(grid.lane == READ, read, jnp.where(grid.lane == TAIL, tail, scale)),
        )
        k_ref[h, c] = keys
        kt_ref[h, c] = keys * tail
        fade_ref[h, c] = fade
        system = fade * mm_nt(keys, keys)
        sys_scr[h, c] = system
        inv_ref[h, c] = eye - jnp.where(grid.differ == 1, system, 0.0)
        rhs_scr[h, c, :, :N] = read * keys
        rhs_scr[h, c, :, N:] = beta * values
        ends[h, c] = jnp.exp(end)
    for level in range(1, 7):
        near = (grid.differ >= (1 << level)) & (grid.differ < (2 << level))
        half = {}
        for i in items:
            half[i] = mm(jnp.where(near, sys_scr[i], 0.0), inv_ref[i])
        for i in items:
            inv_ref[i] = inv_ref[i] - mm(inv_ref[i], half[i])
    for i in items:
        both = mm(inv_ref[i], rhs_scr[i])
        p_ref[i] = both[:, :N]
        y_ref[i] = both[:, N:]
    for i in items:
        maps = mm_tn(kt_ref[i], jnp.concatenate([p_ref[i], y_ref[i]], axis=1))
        t_ref[i] = ends[i] * eye - maps[:, :N]
        o_ref[i] = maps[:, N:]
    for h in range(heads):
        tsh_ref[h] = t_ref[h, 0]
        osh_ref[h] = o_ref[h, 0]
    for c in range(1, count):
        for h in range(heads):
            both = mm(t_ref[h, c], jnp.concatenate([tsh_ref[h], osh_ref[h]], axis=1))
            tsh_ref[h] = both[:, :N]
            osh_ref[h] = both[:, N:] + o_ref[h, c]


def gather_blocks(place_ref, refs, scr, sem, first):
    copies = []
    count = len(refs)
    for s in range(count):
        source = lax.rem(place_ref[0] + count - s, count)
        copies.append(pltpu.make_async_copy(refs[s], scr.at[source], sem.at[first + s]))
    return copies


def scatter_blocks(place_ref, scr, refs, sem, first):
    copies = []
    count = len(refs)
    for s in range(count):
        target = lax.rem(place_ref[0] + s, count)
        copies.append(pltpu.make_async_copy(scr.at[target], refs[s], sem.at[first + s]))
    return copies


def head_rows(ref, heads, h, c):
    return ref[pl.ds(c * C * heads + h, C, stride=heads), :]


def readout_kernel(heads, count, place_ref, g_ref, s_in_ref, k_ref, p_ref, y_ref, t_ref, o_ref, see_ref, run_ref,
                   s_ref, u_ref, dw_ref, dq_ref, *rest):
    outs, (g_scr, dq_scr, sem) = rest[:heads], rest[heads:]
    g_scr[...] = g_ref[...].astype(F32)
    for h in range(heads):
        s_ref[h, 0] = s_in_ref[h].astype(F32)
    for c in range(count):
        for h in range(heads):
            both = mm(jnp.concatenate([t_ref[h, c], p_ref[h, c]], axis=0), s_ref[h, c])
            u_ref[h, c] = y_ref[h, c] - both[N:]
            s_ref[h, c + 1] = both[:N] + o_ref[h, c]
    items = [(h, c) for h in range(heads) for c in range(count)]
    for h, c in items:
        cot = head_rows(g_scr, heads, h, c).astype(BF16)
        both = low_nt(cot, jnp.concatenate([u_ref[h, c], s_ref[h, c]], axis=0))
        dw_ref[h, c] = both[:, :N] * see_ref[h, c]
        dq_ref[h, c] = run_ref[h, c] * both[:, N:]
    for h, c in items:
        grad = mm(dw_ref[h, c], k_ref[h, c]) + dq_ref[h, c]
        dq_ref[h, c] = grad
        dq_scr[h, pl.ds(c * C, C), :] = grad.astype(BF16)
    copies = scatter_blocks(place_ref, dq_scr, outs, sem, 0)
    for copy in copies:
        copy.start()
    for copy in copies:
        copy.wait()


def unit_queries(low):
    raw = low.astype(F32)
    return raw * lax.rsqrt(jnp.mean(raw * raw, axis=1, keepdims=True) + EPS)


def source_kernel(heads, count, place_ref, g_ref, k_ref, p_ref, t_ref, see_ref, run_ref, *rest):
    ins, (q_ref, z_ref, b_ref, bsh_ref, g_scr, q_scr, sem) = rest[:heads], rest[heads:]
    copies = gather_blocks(place_ref, ins, q_scr, sem, 0)
    for copy in copies:
        copy.start()
    g_scr[...] = g_ref[...].astype(F32)
    for copy in copies:
        copy.wait()
    items = [(h, c) for h in range(heads) for c in range(count)]
    weights = {}
    for h, c in items:
        query = unit_queries(q_scr[h, pl.ds(c * C, C), :])
        q_ref[h, c] = query
        weights[h, c] = mm_nt(query, k_ref[h, c]) * see_ref[h, c]
    for h, c in items:
        cot = head_rows(g_scr, heads, h, c).astype(BF16)
        z_ref[h, c] = low_tn(weights[h, c], cot)
        b_ref[h, c] = low_tn(q_ref[h, c] * run_ref[h, c], cot)
    for h, c in items:
        b_ref[h, c] = b_ref[h, c] - mm_tn(p_ref[h, c], z_ref[h, c])
    for h in range(heads):
        bsh_ref[h] = b_ref[h, count - 1]
    for c in range(count - 2, -1, -1):
        for h in range(heads):
            bsh_ref[h] = b_ref[h, c] + mm_tn(t_ref[h, c], bsh_ref[h])


def final_kernel(heads, count, decays_ref, lam_ref, k_ref, kt_ref, inv_ref, t_ref, fade_ref, col_ref,
                 s_ref, u_ref, dw_ref, dq_ref, q_ref, z_ref, b_ref,
                 gk_ref, gv_ref, gb_ref, gd_ref, gk_scr, gv_scr, lam_scr, r_scr, d_scr, rd_scr):
    grid = Grid()
    items = [(h, c) for h in range(heads) for c in range(count)]
    for h in range(heads):
        lam_scr[h, count - 1] = lam_ref[h].astype(F32)
    for c in range(count - 1, 0, -1):
        for h in range(heads):
            lam_scr[h, c - 1] = mm_tn(t_ref[h, c], lam_scr[h, c]) + b_ref[h, c]
    for i in items:
        d_scr[i] = z_ref[i] + mm(kt_ref[i], lam_scr[i])
    for i in items:
        r_scr[i] = mm_tn(inv_ref[i], d_scr[i])
    for h, c in items:
        both = mm_nt(r_scr[h, c], jnp.concatenate([u_ref[h, c], s_ref[h, c]], axis=0))
        d_scr[h, c] = -both[:, :N] * fade_ref[h, c]
        rd_scr[h, c] = -col_ref[h, c, :, READ:READ + 1] * both[:, N:]
    lines = {}
    for h, c in items:
        keys, r = k_ref[h, c], r_scr[h, c]
        cols = col_ref[h, c]
        beta, tail, scale = (cols[:, n:n + 1] for n in (BETA, TAIL, SCALE))
        gb = jnp.sum(r * u_ref[h, c], axis=1, keepdims=True) / beta
        read = mm(d_scr[h, c], keys) + rd_scr[h, c]
        query = q_ref[h, c]
        write = mm_tn(d_scr[h, c], keys) + tail * mm_nt(u_ref[h, c], lam_scr[h, c]) + mm_tn(dw_ref[h, c], query)
        grad = read + write
        gk = scale * (grad - keys * jnp.sum(keys * grad, axis=1, keepdims=True))
        gv = beta * r
        base = c * C * 2 * heads
        for m in range(2):
            rows = pl.ds(base + m * heads + h, C, stride=2 * heads)
            gk_scr[rows, :] = gk[m * C:(m + 1) * C]
            gv_scr[rows, :] = gv[m * C:(m + 1) * C]
        pulls = keys * (read - write)
        pulls = jnp.sum(pulls[:C] + pulls[C:] + query * dq_ref[h, c], axis=1, keepdims=True)
        after = grid.row_pos[:C] >= grid.lane_pos[:C]
        total = jnp.sum(
            jnp.sum(s_ref[h, c + 1] * lam_scr[h, c], axis=0, keepdims=True), axis=1, keepdims=True
        )
        gd = jnp.sum(jnp.where(after, pulls, 0.0), axis=0, keepdims=True) + total
        half = C * (c % 2)
        mine = (grid.lane[:1] >= half) & (grid.lane[:1] < half + C)
        lines[h, c, 2] = jnp.where(mine, gd, 0.0)
        for m in range(2):
            pick = (grid.lane - half == grid.row - m * C) & (grid.row >= m * C) & (grid.row < (m + 1) * C)
            lines[h, c, m] = jnp.sum(jnp.where(pick, gb, 0.0), axis=0, keepdims=True)
    for h in range(heads):
        for p in range(count // 2):
            lanes = pl.ds(p * N, N)
            for m in range(2):
                gb_ref[m, pl.ds(h, 1), lanes] = lines[h, 2 * p, m] + lines[h, 2 * p + 1, m]
            gd_ref[pl.ds(h, 1), lanes] = (lines[h, 2 * p, 2] + lines[h, 2 * p + 1, 2]) / decays_ref[pl.ds(h, 1), lanes]
    gk_ref[...] = gk_scr[...].astype(BF16)
    gv_ref[...] = gv_scr[...].astype(BF16)


ANY = pl.BlockSpec(memory_space=pl.ANY)
SCALAR = pl.BlockSpec(memory_space=pltpu.SMEM)
VM = pl.BlockSpec(memory_space=pltpu.VMEM)


def shaped(shape, dtype=F32):
    return jax.ShapeDtypeStruct(shape, dtype)


def single(body, name, in_specs, outs, out_specs, scratch, flops):
    return pl.pallas_call(
        body,
        name=name,
        in_specs=in_specs,
        out_shape=outs,
        out_specs=out_specs,
        scratch_shapes=scratch,
        compiler_params=pltpu.CompilerParams(vmem_limit_bytes=LIMIT),
        cost_estimate=pl.CostEstimate(flops=flops, bytes_accessed=4 << 20, transcendentals=0),
    )


def delta_local(dk, dv, betas, decays):
    heads, rows = decays.shape
    count = rows // C
    square, thin, one = (shaped((heads,) + tail) for tail in ((count, N, N), (count, C, N), (N, N)))
    outs = [square] * 8 + [thin] * 2 + [square] + [one] * 2
    return single(
        functools.partial(local_kernel, heads, count), "delta_local",
        [ANY, ANY, VM, VM], outs, [VM] * len(outs),
        [pltpu.VMEM((2,) + dk.shape, BF16)] + [pltpu.VMEM(dk.shape, F32)] * 2
        + [pltpu.VMEM((heads, count, N, N), F32), pltpu.VMEM((heads, count, N, 2 * N), F32),
           pltpu.SemaphoreType.DMA((2,))],
        10 << 30,
    )(dk, dv, betas, decays)


def delta_readout(place, g, entry, k, p, y, t, o, see, run):
    heads, count = k.shape[:2]
    rows = count * C
    square, thin = (shaped((heads,) + tail) for tail in ((count, N, N), (count, C, N)))
    outs = [shaped((heads, count + 1, N, N)), square, thin, thin]
    return single(
        functools.partial(readout_kernel, heads, count), "delta_readout",
        [SCALAR] + [VM] * 9, outs + [shaped((rows, N), BF16)] * heads, [VM] * 4 + [ANY] * heads,
        [pltpu.VMEM(g.shape, F32), pltpu.VMEM((heads, rows, N), BF16), pltpu.SemaphoreType.DMA((heads,))],
        3 << 30,
    )(place, g, entry, k, p, y, t, o, see, run)


def delta_source(place, g, k, p, t, see, run, attended):
    heads, count = k.shape[:2]
    rows = count * C
    square, thin = (shaped((heads,) + tail) for tail in ((count, N, N), (count, C, N)))
    return single(
        functools.partial(source_kernel, heads, count), "delta_source",
        [SCALAR] + [VM] * 6 + [ANY] * heads,
        [thin, square, square, shaped((heads, N, N))], [VM] * 4,
        [pltpu.VMEM(g.shape, F32), pltpu.VMEM((heads, rows, N), BF16), pltpu.SemaphoreType.DMA((heads,))],
        3 << 30,
    )(place, g, k, p, t, see, run, *attended)


def delta_final(betas, decays, lam, k, kt, inv, t, fade, col, s, u, dw, dq, q, z, b):
    heads, count = k.shape[:2]
    wide = (2 * count * C * heads, N)
    return single(
        functools.partial(final_kernel, heads, count), "delta_final",
        [VM] * 15,
        [shaped(wide, BF16), shaped(wide, BF16), shaped(betas.shape), shaped(decays.shape)], [VM] * 4,
        [pltpu.VMEM(wide, F32)] * 2 + [pltpu.VMEM((heads, count, N, N), F32)] * 4,
        8 << 30,
    )(decays, lam, k, kt, inv, t, fade, col, s, u, dw, dq, q, z, b)


def rounds(refs, index, count, sign):
    return [lax.rem(index + (s if sign > 0 else count - s), count) for s in range(count)]


def send_kernel(count, place_ref, q_ref, k_ref, v_ref, *rest):
    outs, (low, scr, sem) = rest[:count], rest[count:]
    heads = count
    rows = q_ref.shape[0] // heads
    copies = [pltpu.make_async_copy(ref, low.at[m], sem.at[m]) for m, ref in enumerate((q_ref, k_ref, v_ref))]
    for copy in copies:
        copy.start()
    for m in range(3):
        copies[m].wait()
        scr[m] = low[m].astype(F32)
        for s in range(count):
            head = lax.rem(place_ref[0] + s, count)
            outs[s][m] = scr[m, pl.ds(head, rows, stride=heads), :].astype(BF16)


def take_kernel(count, place_ref, *rest):
    ins, outs, (scr,) = rest[:count], rest[count:count + 3], rest[count + 3:]
    heads = count
    rows = outs[0].shape[0] // heads
    for m in range(3):
        for s in range(count):
            head = lax.rem(place_ref[0] + count - s, count)
            scr[pl.ds(head, rows, stride=heads), :] = ins[s][m].astype(F32)
        outs[m][...] = scr[...].astype(BF16)


def attend_kernel(count, scale, place_ref, *rest):
    ins, (prob_ref, mixed_ref), outs = rest[:count], rest[count:count + 2], rest[count + 2:2 * count + 2]
    scr, att_scr, sem = rest[2 * count + 2:]
    copies = gather_blocks(place_ref, ins, scr, sem, 0)
    for copy in copies:
        copy.start()
    for copy in copies:
        copy.wait()
    rows = scr.shape[2]
    causal = iota((rows, rows), 0) <= iota((rows, rows), 1)
    for i in range(count):
        query = scr[i, 0]
        pieces = []
        for j in range(i + 1):
            score = contract(scr[j, 1], query, 1, 1) * scale
            pieces.append(jnp.where(causal, score, -jnp.inf) if j == i else score)
        top = pieces[0].max(axis=0, keepdims=True)
        for piece in pieces[1:]:
            top = jnp.maximum(top, piece.max(axis=0, keepdims=True))
        pieces = [jnp.exp(piece - top) for piece in pieces]
        total = pieces[0].sum(axis=0, keepdims=True)
        for piece in pieces[1:]:
            total = total + piece.sum(axis=0, keepdims=True)
        mixed = None
        for j, piece in enumerate(pieces):
            low = (piece / total).astype(BF16)
            prob_ref[i * (i + 1) // 2 + j] = low
            term = contract(low, scr[j, 2], 0, 0)
            mixed = term if mixed is None else mixed + term
        mixed_ref[i] = mixed
        att_scr[i] = mixed.astype(BF16)
    copies = scatter_blocks(place_ref, att_scr, outs, sem, 0)
    for copy in copies:
        copy.start()
    for copy in copies:
        copy.wait()


def attend_back_kernel(count, scale, place_ref, prob_ref, mixed_ref, *rest):
    ins, grads, outs = rest[:count], rest[count:2 * count], rest[2 * count:3 * count]
    scr, g_scr, out_scr, acc, sem = rest[3 * count:]
    copies = gather_blocks(place_ref, ins, scr, sem, 0) + gather_blocks(place_ref, grads, g_scr, sem, count)
    for copy in copies:
        copy.start()
    for copy in copies:
        copy.wait()
    rows = scr.shape[2]
    ones = jnp.ones((8, N), F32)
    for i in range(count):
        mixed = mixed_ref[i]
        low = mixed.astype(BF16).astype(F32)
        grad = g_scr[i].astype(F32)
        inv = lax.rsqrt(jnp.mean(low * low, axis=1, keepdims=True) + EPS)
        pull = inv * (grad - low * (inv * inv * jnp.mean(low * grad, axis=1, keepdims=True)))
        pull = pull.astype(BF16)
        dots = mm_nt(ones, pull.astype(F32) * mixed)[:1]
        query = scr[i, 0]
        gq = None
        for j in range(i + 1):
            prob = prob_ref[i * (i + 1) // 2 + j]
            gp = contract(scr[j, 2], pull, 1, 1)
            gs = (prob.astype(F32) * (gp - dots) * scale).astype(BF16)
            term = contract(gs, scr[j, 1], 0, 0)
            gq = term if gq is None else gq + term
            gk = contract(gs, query, 1, 0)
            gv = contract(prob, pull, 1, 0)
            if i == j:
                acc[j, 0] = gk
                acc[j, 1] = gv
            else:
                acc[j, 0] = acc[j, 0] + gk
                acc[j, 1] = acc[j, 1] + gv
        out_scr[i, 0] = gq.astype(BF16)
    for j in range(count):
        out_scr[j, 1] = acc[j, 0].astype(BF16)
        out_scr[j, 2] = acc[j, 1].astype(BF16)
    copies = scatter_blocks(place_ref, out_scr, outs, sem, 0)
    for copy in copies:
        copy.start()
    for copy in copies:
        copy.wait()


def send_heads(place, q, k, v, count):
    rows = q.shape[0] // count
    return single(
        functools.partial(send_kernel, count), "send_heads",
        [SCALAR, ANY, ANY, ANY], [shaped((3, rows, N), BF16)] * count, [VM] * count,
        [pltpu.VMEM((3,) + q.shape, BF16), pltpu.VMEM((3,) + q.shape, F32), pltpu.SemaphoreType.DMA((3,))],
        1 << 28,
    )(place, q, k, v)


def take_heads(place, parts):
    count = len(parts)
    rows = parts[0].shape[1]
    wide = (rows * count, N)
    return single(
        functools.partial(take_kernel, count), "take_heads",
        [SCALAR] + [VM] * count, [shaped(wide, BF16)] * 3, [VM] * 3,
        [pltpu.VMEM(wide, F32)], 1 << 28,
    )(place, *parts)


def attend(place, parts, scale):
    count = len(parts)
    rows = parts[0].shape[1]
    tri = count * (count + 1) // 2
    return single(
        functools.partial(attend_kernel, count, scale), "attend",
        [SCALAR] + [ANY] * count,
        [shaped((tri, rows, rows), BF16), shaped((count, rows, N))] + [shaped((rows, N), BF16)] * count,
        [VM, VM] + [ANY] * count,
        [pltpu.VMEM((count, 3, rows, N), BF16), pltpu.VMEM((count, rows, N), BF16),
         pltpu.SemaphoreType.DMA((count,))], 2 << 30,
    )(place, *parts)


def attend_back(place, prob, mixed, parts, grads, scale):
    count = len(parts)
    rows = parts[0].shape[1]
    return single(
        functools.partial(attend_back_kernel, count, scale), "attend_back",
        [SCALAR, VM, VM] + [ANY] * (2 * count),
        [shaped((3, rows, N), BF16)] * count, [ANY] * count,
        [pltpu.VMEM((count, 3, rows, N), BF16), pltpu.VMEM((count, rows, N), BF16),
         pltpu.VMEM((count, 3, rows, N), BF16), pltpu.VMEM((count, 2, rows, N), F32),
         pltpu.SemaphoreType.DMA((2 * count,))], 4 << 30,
    )(place, prob, mixed, *parts, *grads)


PRECISE = lax.Precision.HIGHEST


def shifted(value, axis, steps):
    count = lax.axis_size(axis)
    initial, last = (max(0, -steps), min(count, count - steps))
    return lax.ppermute(value, axis, [(source, source + steps) for source in range(initial, last)])


def rotated(parts, axis):
    count = len(parts)
    moved = [parts[0]]
    for s in range(1, count):
        moved.append(lax.ppermute(parts[s], axis, [(d, (d + s) % count) for d in range(count)]))
    return moved


def apply_map(matrix, state):
    return jnp.einsum("hij,hjk->hik", matrix, state, precision=PRECISE)


def entering(matrix, offset, axis, step):
    count = lax.axis_size(axis)
    if count <= 4:
        state = shifted(offset.astype(BF16), axis, step)
        for hop in range(count - 2):
            state = shifted((apply_map(matrix, state.astype(F32)) + offset).astype(BF16), axis, step)
        return state
    place = lax.axis_index(axis)
    place = place if step > 0 else count - 1 - place
    eye = jnp.eye(matrix.shape[-1], dtype=F32)
    reach = 1
    while reach < count:
        before, start = (shifted(matrix, axis, step * reach), shifted(offset, axis, step * reach))
        before = before + jnp.where(place < reach, eye, 0.0)
        offset = apply_map(matrix, start) + offset
        matrix = apply_map(matrix, before)
        reach *= 2
    return shifted(offset, axis, step).astype(BF16)


def visible_pairs(rows, span):
    relative = jnp.arange((span + 1) * rows, dtype=jnp.int32) - span * rows
    local = jnp.arange(rows, dtype=jnp.int32)
    return (
        (relative[None, :] <= local[:, None])
        & (relative[None, :] > local[:, None] - WINDOW)
        & (lax.axis_index("seq") * rows + relative[None, :] >= 0)
    )


def window_forward(queries, keys, values, scale):
    rows = queries.shape[0]
    span = -(-WINDOW // rows)
    couple = jnp.stack([keys, values])
    earlier = [shifted(couple, "seq", step + 1) for step in range(min(span, lax.axis_size("seq") - 1))]
    span = len(earlier)
    ordered = earlier[::-1] + [couple]
    window_keys = jnp.concatenate([piece[0] for piece in ordered], axis=0)
    window_values = jnp.concatenate([piece[1] for piece in ordered], axis=0)
    visible = visible_pairs(rows, span)
    scores = jnp.einsum("qhe,khe->hqk", queries, window_keys, preferred_element_type=F32) * scale
    top = jnp.max(jnp.where(visible, scores, -jnp.inf), axis=-1)
    lifted = jnp.where(visible, jnp.exp(jnp.where(visible, scores - top[:, :, None], 0.0)), 0.0)
    attention = lifted / jnp.sum(lifted, axis=-1)[:, :, None]
    mixed = jnp.einsum(
        "hqk,khe->qhe", attention.astype(BF16), window_values, preferred_element_type=F32
    )
    return window_keys, window_values, attention, mixed, span


def window_backward(queries, window_keys, window_values, attention, mixed, span, unit_grad, scale):
    rows = queries.shape[0]
    low = mixed.astype(BF16).astype(F32)
    grad = unit_grad.astype(F32)
    inv = lax.rsqrt(jnp.mean(low * low, axis=-1, keepdims=True) + EPS)
    pull = inv * (grad - low * (inv * inv * jnp.mean(low * grad, axis=-1, keepdims=True)))
    pull = pull.astype(BF16)
    row_dots = jnp.sum(pull.astype(F32) * mixed, axis=-1).T
    grad_attention = jnp.einsum("qhe,khe->hqk", pull, window_values, preferred_element_type=F32)
    grad_scores = (attention * (grad_attention - row_dots[:, :, None]) * scale).astype(BF16)
    grad_queries = jnp.einsum(
        "hqk,khe->qhe", grad_scores, window_keys, preferred_element_type=F32
    ).astype(BF16)
    key_parts = jnp.einsum("hqk,qhe->khe", grad_scores, queries, preferred_element_type=F32)
    value_parts = jnp.einsum("hqk,qhe->khe", attention.astype(BF16), pull, preferred_element_type=F32)
    gathered = jnp.stack([key_parts[span * rows:], value_parts[span * rows:]])
    for later in range(1, span + 1):
        first = (span - later) * rows
        piece = jnp.stack([key_parts[first:first + rows], value_parts[first:first + rows]])
        gathered = gathered + shifted(piece, "seq", -later)
    return grad_queries, gathered[0].astype(BF16), gathered[1].astype(BF16)


def body(queries, keys, values, delta_keys, delta_values, betas, decays, grad_out):
    rows, heads, width = queries.shape
    scale = 1.0 / math.sqrt(width)
    count = lax.axis_size("seq")
    by_head = heads == count and WINDOW >= count * rows

    def flat(array):
        return array.reshape(-1, width)

    place = lax.axis_index("seq").astype(jnp.int32).reshape(1) if by_head else jnp.zeros((1,), jnp.int32)
    pairs = flat(delta_keys)
    if by_head:
        parts = send_heads(place, flat(queries), flat(keys), flat(values), count)
        pairs, parts = lax.optimization_barrier((pairs, parts))
        parts = rotated(parts, "seq")
    cot = flat(grad_out)
    k, kt, inverse, p, y, t, o, fade, see, run, col, shard_t, shard_o = delta_local(
        pairs, flat(delta_values), betas, decays
    )
    entry = entering(shard_t, shard_o, "seq", 1)
    if by_head:
        prob, mixed, *attended = attend(place, parts, scale)
        attended = rotated(attended, "seq")
    else:
        saved = window_forward(queries, keys, values, scale)
        low = saved[3].astype(BF16)
        attended = [low[:, (heads - s) % heads] for s in range(heads)]
    s, u, dw, dq, *pulls = delta_readout(place, cot, entry, k, p, y, t, o, see, run)
    if by_head:
        pulls = rotated(pulls, "seq")
        outs = rotated(attend_back(place, prob, mixed, parts, pulls, scale), "seq")
    else:
        grads = window_backward(queries, *saved, jnp.stack(pulls, axis=1), scale)
    q, z, b, shard_source = delta_source(place, cot, k, p, t, see, run, attended)
    leaving = entering(jnp.swapaxes(shard_t, 1, 2), shard_source, "seq", -1)
    grad_keys, grad_values, grad_betas, grad_decays = delta_final(
        betas, decays, leaving, k, kt, inverse, t, fade, col, s, u, dw, dq, q, z, b
    )
    if by_head:
        outs, grad_keys = lax.optimization_barrier((outs, grad_keys))
        grads = [array.reshape(rows, heads, width) for array in take_heads(place, outs)]
    pair = (rows, 2, heads, width)
    return (*grads, grad_keys.reshape(pair), grad_values.reshape(pair), grad_betas, grad_decays)


def solution(mesh):
    row = P(("parts", "seq"), "head", None)
    pair = P(("parts", "seq"), None, "head", None)
    beta = P(None, "head", ("parts", "seq"))
    decay = P("head", ("parts", "seq"))
    return jax.shard_map(
        body,
        mesh=mesh,
        in_specs=(row, row, row, pair, pair, beta, decay, row),
        out_specs=(row, row, row, pair, pair, beta, decay),
        check_vma=False,
    )
```

```python
import functools, math
import jax
import jax.numpy as jnp
from jax import lax
from jax.experimental import pallas as pl
from jax.experimental.pallas import tpu as pltpu
from jax.sharding import PartitionSpec as P

WINDOW = 1024

F32 = jnp.float32
BF16 = jnp.bfloat16
EPS = 1e-06
C = 64
N = 128
LIMIT = 16 * 1024 * 1024
SENDLIMIT = 58 * 1024 * 1024
SENDFLOPS = 20 << 30


def split(a):
    high = a.astype(BF16)
    return high, (a - high.astype(F32)).astype(BF16)


def contract(a, b, ca, cb):
    return lax.dot_general(a, b, (((ca,), (cb,)), ((), ())), preferred_element_type=F32)


def mm(a, b):
    ah, al = split(a)
    bh, bl = split(b)
    wide = jnp.concatenate([bh, bl], axis=1)
    both = contract(jnp.concatenate([ah, al], axis=1), jnp.concatenate([wide, wide], axis=0), 1, 0)
    half = b.shape[1]
    return both[:, :half] + both[:, half:]


def mm_nt(a, b):
    ah, al = split(a)
    bh, bl = split(b)
    tall = jnp.concatenate([bh, bl], axis=0)
    both = contract(jnp.concatenate([ah, al], axis=1), jnp.concatenate([tall, tall], axis=1), 1, 1)
    half = b.shape[0]
    return both[:, :half] + both[:, half:]


def mm_tn(a, b):
    ah, al = split(a)
    bh, bl = split(b)
    wide = jnp.concatenate([bh, bl], axis=1)
    both = contract(jnp.concatenate([ah, al], axis=0), jnp.concatenate([wide, wide], axis=0), 0, 0)
    half = b.shape[1]
    return both[:, :half] + both[:, half:]


def low_nt(low, b):
    bh, bl = split(b)
    both = contract(low, jnp.concatenate([bh, bl], axis=0), 1, 1)
    half = b.shape[0]
    return both[:, :half] + both[:, half:]


def low_tn(a, low):
    ah, al = split(a)
    return contract(jnp.concatenate([ah, al], axis=0), jnp.concatenate([low, low], axis=0), 0, 0)


def iota(shape, axis):
    return lax.broadcasted_iota(jnp.int32, shape, axis)


class Grid:
    def __init__(self):
        self.row = iota((N, N), 0)
        self.lane = iota((N, N), 1)
        self.row_pos = self.row & (C - 1)
        self.lane_pos = self.lane & (C - 1)
        key_row = 2 * self.row_pos + (self.row >> 6)
        key_lane = 2 * self.lane_pos + (self.lane >> 6)
        self.strict = key_row > key_lane
        self.differ = key_row ^ key_lane
        self.diag = self.row == self.lane

    def to_row(self, column):
        return jnp.sum(jnp.where(self.diag, column, 0.0), axis=0, keepdims=True)

    def to_column(self, line):
        return jnp.sum(jnp.where(self.diag, line, 0.0), axis=1, keepdims=True)


def gates(grid, betas_ref, decays_ref, h, c):
    pair, half = c // 2, C * (c % 2)
    lanes = pl.ds(pair * N, N)
    first = betas_ref[0, pl.ds(h, 1), lanes]
    second = betas_ref[1, pl.ds(h, 1), lanes]
    logs = jnp.log(decays_ref[pl.ds(h, 1), lanes])
    offset = grid.lane - half
    chosen = jnp.where(grid.row < C, first, second)
    beta = jnp.sum(jnp.where(offset == grid.row_pos, chosen, 0.0), axis=1, keepdims=True)
    seen = (offset >= 0) & (offset <= grid.row_pos)
    run = jnp.sum(jnp.where(seen, logs, 0.0), axis=1, keepdims=True)
    inside = (offset[:1] >= 0) & (offset[:1] < C)
    end = jnp.sum(jnp.where(inside, logs, 0.0), axis=1, keepdims=True)
    return beta, run, grid.to_row(run), end


def pair_rows(ref, heads, h, c):
    base = c * C * 2 * heads
    return jnp.concatenate(
        [
            ref[pl.ds(base + h, C, stride=2 * heads), :],
            ref[pl.ds(base + heads + h, C, stride=2 * heads), :],
        ],
        axis=0,
    )


BETA, READ, TAIL, SCALE = range(4)


def pair_product(ah, al, bh, bl):
    wide = jnp.concatenate([bh, bl], axis=1)
    both = contract(jnp.concatenate([ah, al], axis=1), jnp.concatenate([wide, wide], axis=0), 1, 0)
    half = bh.shape[1]
    return both[:, :half] + both[:, half:]


def local_kernel(heads, count, dk_ref, dv_ref, betas_ref, decays_ref,
                 k_ref, kt_ref, inv_ref, p_ref, y_ref, t_ref, o_ref, fade_ref, see_ref, run_ref, col_ref,
                 tsh_ref, osh_ref, low_ref,
                 keys_scr, values_scr, sys_scr, full_scr, split_scr, half_scr, rhs_scr):
    grid = Grid()
    eye = jnp.where(grid.diag, 1.0, 0.0)
    items = [(h, c) for h in range(heads) for c in range(count)]
    keys_scr[...] = dk_ref[...].astype(F32)
    values_scr[...] = dv_ref[...].astype(F32)
    ends = {}
    for h, c in items:
        raw = pair_rows(keys_scr, heads, h, c)
        values = pair_rows(values_scr, heads, h, c)
        scale = lax.rsqrt(jnp.sum(raw * raw, axis=1, keepdims=True) + EPS)
        keys = raw * scale
        beta, run, line, end = gates(grid, betas_ref, decays_ref, h, c)
        tail = jnp.exp(end - run)
        read = beta * jnp.exp(run)
        fade = beta * jnp.where(grid.strict, jnp.exp(jnp.minimum(run - line, 0.0)), 0.0)
        seen = grid.lane_pos[:C] <= grid.row_pos[:C]
        see_ref[h, c] = jnp.where(seen, jnp.exp(jnp.minimum(run[:C] - line, 0.0)), 0.0)
        run_ref[h, c] = jnp.broadcast_to(jnp.exp(run[:C]), (C, N))
        col_ref[h, c] = jnp.where(
            grid.lane == BETA, beta,
            jnp.where(grid.lane == READ, read, jnp.where(grid.lane == TAIL, tail, scale)),
        )
        k_ref[h, c] = keys
        kt_ref[h, c] = keys * tail
        fade_ref[h, c] = fade
        system = fade * mm_nt(keys, keys)
        sys_scr[0, h, c], sys_scr[1, h, c] = split(system)
        inverse = eye - jnp.where(grid.differ == 1, system, 0.0)
        inv_ref[h, c] = inverse
        split_scr[0, h, c], split_scr[1, h, c] = split(inverse)
        rhs_scr[h, c, :, :N] = read * keys
        rhs_scr[h, c, :, N:] = beta * values
        ends[h, c] = jnp.exp(end)
    for level in range(1, 7):
        near = (grid.differ >= (1 << level)) & (grid.differ < (2 << level))
        near = jnp.where(near, 1.0, 0.0).astype(BF16)
        for h, c in items:
            half = pair_product(
                sys_scr[0, h, c] * near, sys_scr[1, h, c] * near, split_scr[0, h, c], split_scr[1, h, c]
            )
            half_scr[0, h, c], half_scr[1, h, c] = split(half)
        for h, c in items:
            inverse = inv_ref[h, c] - pair_product(
                split_scr[0, h, c], split_scr[1, h, c], half_scr[0, h, c], half_scr[1, h, c]
            )
            inv_ref[h, c] = inverse
            split_scr[0, h, c], split_scr[1, h, c] = split(inverse)
    for h, c in items:
        both = pair_product(split_scr[0, h, c], split_scr[1, h, c], *split(rhs_scr[h, c]))
        p_ref[h, c] = both[:, :N]
        y_ref[h, c] = both[:, N:]
    for i in items:
        maps = mm_tn(kt_ref[i], jnp.concatenate([p_ref[i], y_ref[i]], axis=1))
        t_ref[i] = ends[i] * eye - maps[:, :N]
        o_ref[i] = maps[:, N:]
    for h in range(heads):
        tsh_ref[h] = t_ref[h, 0]
        osh_ref[h] = o_ref[h, 0]
    for c in range(1, count):
        for h in range(heads):
            both = mm(t_ref[h, c], jnp.concatenate([tsh_ref[h], osh_ref[h]], axis=1))
            tsh_ref[h] = both[:, :N]
            osh_ref[h] = both[:, N:] + o_ref[h, c]
    for h in range(heads):
        low_ref[0, h] = osh_ref[h].astype(BF16)
        low_ref[1, h] = tsh_ref[h].astype(BF16)


def gather_blocks(place_ref, refs, scr, sem, first):
    copies = []
    count = len(refs)
    for s in range(count):
        source = lax.rem(place_ref[0] + count - s, count)
        copies.append(pltpu.make_async_copy(refs[s], scr.at[source], sem.at[first + s]))
    return copies


def scatter_blocks(place_ref, scr, refs, sem, first):
    copies = []
    count = len(refs)
    for s in range(count):
        target = lax.rem(place_ref[0] + s, count)
        copies.append(pltpu.make_async_copy(scr.at[target], refs[s], sem.at[first + s]))
    return copies


def head_rows(ref, heads, h, c):
    return ref[pl.ds(c * C * heads + h, C, stride=heads), :]


def readout_kernel(heads, count, place_ref, g_ref, near_ref, far_ref, k_ref, p_ref, y_ref, t_ref, o_ref, see_ref, run_ref,
                   s_ref, u_ref, dw_ref, dq_ref, *rest):
    outs, (g_scr, dq_scr, sem) = rest[:heads], rest[heads:]
    g_scr[...] = g_ref[...].astype(F32)
    for h in range(heads):
        s_ref[h, 0] = near_ref[0, h].astype(F32) + contract(near_ref[1, h], far_ref[h], 1, 0)
    for c in range(count):
        for h in range(heads):
            both = mm(jnp.concatenate([t_ref[h, c], p_ref[h, c]], axis=0), s_ref[h, c])
            u_ref[h, c] = y_ref[h, c] - both[N:]
            s_ref[h, c + 1] = both[:N] + o_ref[h, c]
    items = [(h, c) for h in range(heads) for c in range(count)]
    for h, c in items:
        cot = head_rows(g_scr, heads, h, c).astype(BF16)
        both = low_nt(cot, jnp.concatenate([u_ref[h, c], s_ref[h, c]], axis=0))
        dw_ref[h, c] = both[:, :N] * see_ref[h, c]
        dq_ref[h, c] = run_ref[h, c] * both[:, N:]
    for h, c in items:
        grad = mm(dw_ref[h, c], k_ref[h, c]) + dq_ref[h, c]
        dq_ref[h, c] = grad
        dq_scr[h, pl.ds(c * C, C), :] = grad.astype(BF16)
    copies = scatter_blocks(place_ref, dq_scr, outs, sem, 0)
    for copy in copies:
        copy.start()
    for copy in copies:
        copy.wait()


def unit_queries(low):
    raw = low.astype(F32)
    return raw * lax.rsqrt(jnp.mean(raw * raw, axis=1, keepdims=True) + EPS)


def source_kernel(heads, count, place_ref, g_ref, k_ref, p_ref, t_ref, see_ref, run_ref, map_ref, *rest):
    ins, (q_ref, z_ref, b_ref, bsh_ref, low_ref, g_scr, q_scr, sem) = rest[:heads], rest[heads:]
    copies = gather_blocks(place_ref, ins, q_scr, sem, 0)
    for copy in copies:
        copy.start()
    g_scr[...] = g_ref[...].astype(F32)
    for copy in copies:
        copy.wait()
    items = [(h, c) for h in range(heads) for c in range(count)]
    weights = {}
    for h, c in items:
        query = unit_queries(q_scr[h, pl.ds(c * C, C), :])
        q_ref[h, c] = query
        weights[h, c] = mm_nt(query, k_ref[h, c]) * see_ref[h, c]
    for h, c in items:
        cot = head_rows(g_scr, heads, h, c).astype(BF16)
        z_ref[h, c] = low_tn(weights[h, c], cot)
        b_ref[h, c] = low_tn(q_ref[h, c] * run_ref[h, c], cot)
    for h, c in items:
        b_ref[h, c] = b_ref[h, c] - mm_tn(p_ref[h, c], z_ref[h, c])
    for h in range(heads):
        bsh_ref[h] = b_ref[h, count - 1]
    for c in range(count - 2, -1, -1):
        for h in range(heads):
            bsh_ref[h] = b_ref[h, c] + mm_tn(t_ref[h, c], bsh_ref[h])
    for h in range(heads):
        low_ref[0, h] = bsh_ref[h].astype(BF16)
        low_ref[1, h] = map_ref[1, h]


def final_kernel(heads, count, decays_ref, near_ref, far_ref, k_ref, kt_ref, inv_ref, t_ref, fade_ref, col_ref,
                 s_ref, u_ref, dw_ref, dq_ref, q_ref, z_ref, b_ref,
                 gk_ref, gv_ref, gb_ref, gd_ref, gk_scr, gv_scr, lam_scr, r_scr, d_scr, rd_scr):
    grid = Grid()
    items = [(h, c) for h in range(heads) for c in range(count)]
    for h in range(heads):
        lam_scr[h, count - 1] = near_ref[0, h].astype(F32) + contract(near_ref[1, h], far_ref[h], 0, 0)
    for c in range(count - 1, 0, -1):
        for h in range(heads):
            lam_scr[h, c - 1] = mm_tn(t_ref[h, c], lam_scr[h, c]) + b_ref[h, c]
    for i in items:
        d_scr[i] = z_ref[i] + mm(kt_ref[i], lam_scr[i])
    for i in items:
        r_scr[i] = mm_tn(inv_ref[i], d_scr[i])
    for h, c in items:
        both = mm_nt(r_scr[h, c], jnp.concatenate([u_ref[h, c], s_ref[h, c]], axis=0))
        d_scr[h, c] = -both[:, :N] * fade_ref[h, c]
        rd_scr[h, c] = -col_ref[h, c, :, READ:READ + 1] * both[:, N:]
    lines = {}
    for h, c in items:
        keys, r = k_ref[h, c], r_scr[h, c]
        cols = col_ref[h, c]
        beta, tail, scale = (cols[:, n:n + 1] for n in (BETA, TAIL, SCALE))
        gb = jnp.sum(r * u_ref[h, c], axis=1, keepdims=True) / beta
        read = mm(d_scr[h, c], keys) + rd_scr[h, c]
        query = q_ref[h, c]
        write = mm_tn(d_scr[h, c], keys) + tail * mm_nt(u_ref[h, c], lam_scr[h, c]) + mm_tn(dw_ref[h, c], query)
        grad = read + write
        gk = scale * (grad - keys * jnp.sum(keys * grad, axis=1, keepdims=True))
        gv = beta * r
        base = c * C * 2 * heads
        for m in range(2):
            rows = pl.ds(base + m * heads + h, C, stride=2 * heads)
            gk_scr[rows, :] = gk[m * C:(m + 1) * C]
            gv_scr[rows, :] = gv[m * C:(m + 1) * C]
        pulls = keys * (read - write)
        pulls = jnp.sum(pulls[:C] + pulls[C:] + query * dq_ref[h, c], axis=1, keepdims=True)
        after = grid.row_pos[:C] >= grid.lane_pos[:C]
        total = jnp.sum(
            jnp.sum(s_ref[h, c + 1] * lam_scr[h, c], axis=0, keepdims=True), axis=1, keepdims=True
        )
        gd = jnp.sum(jnp.where(after, pulls, 0.0), axis=0, keepdims=True) + total
        half = C * (c % 2)
        mine = (grid.lane[:1] >= half) & (grid.lane[:1] < half + C)
        lines[h, c, 2] = jnp.where(mine, gd, 0.0)
        for m in range(2):
            pick = (grid.lane - half == grid.row - m * C) & (grid.row >= m * C) & (grid.row < (m + 1) * C)
            lines[h, c, m] = jnp.sum(jnp.where(pick, gb, 0.0), axis=0, keepdims=True)
    for h in range(heads):
        for p in range(count // 2):
            lanes = pl.ds(p * N, N)
            for m in range(2):
                gb_ref[m, pl.ds(h, 1), lanes] = lines[h, 2 * p, m] + lines[h, 2 * p + 1, m]
            gd_ref[pl.ds(h, 1), lanes] = (lines[h, 2 * p, 2] + lines[h, 2 * p + 1, 2]) / decays_ref[pl.ds(h, 1), lanes]
    gk_ref[...] = gk_scr[...].astype(BF16)
    gv_ref[...] = gv_scr[...].astype(BF16)


ANY = pl.BlockSpec(memory_space=pl.ANY)
HBM = pl.BlockSpec(memory_space=pltpu.HBM)
SCALAR = pl.BlockSpec(memory_space=pltpu.SMEM)
VM = pl.BlockSpec(memory_space=pltpu.VMEM)


def shaped(shape, dtype=F32):
    return jax.ShapeDtypeStruct(shape, dtype)


def single(body, name, in_specs, outs, out_specs, scratch, flops, limit=LIMIT):
    return pl.pallas_call(
        body,
        name=name,
        in_specs=in_specs,
        out_shape=outs,
        out_specs=out_specs,
        scratch_shapes=scratch,
        compiler_params=pltpu.CompilerParams(vmem_limit_bytes=limit),
        cost_estimate=pl.CostEstimate(flops=flops, bytes_accessed=4 << 20, transcendentals=0),
    )


def delta_local(dk, dv, betas, decays):
    heads, rows = decays.shape
    count = rows // C
    square, thin, one = (shaped((heads,) + tail) for tail in ((count, N, N), (count, C, N), (N, N)))
    outs = [square] * 8 + [thin] * 2 + [square] + [one] * 2 + [shaped((2, heads, N, N), BF16)]
    halves = pltpu.VMEM((2, heads, count, N, N), BF16)
    return single(
        functools.partial(local_kernel, heads, count), "delta_local",
        [VM] * 4, outs, [VM] * len(outs),
        [pltpu.VMEM(dk.shape, F32)] * 2 + [halves, pltpu.VMEM(square.shape, F32), halves, halves]
        + [pltpu.VMEM((heads, count, N, 2 * N), F32)],
        10 << 30,
    )(dk, dv, betas, decays)


def delta_readout(place, g, near, far, k, p, y, t, o, see, run):
    heads, count = k.shape[:2]
    rows = count * C
    square, thin = (shaped((heads,) + tail) for tail in ((count, N, N), (count, C, N)))
    outs = [shaped((heads, count + 1, N, N)), square, thin, thin]
    return single(
        functools.partial(readout_kernel, heads, count), "delta_readout",
        [SCALAR] + [VM] * 10, outs + [shaped((rows, N), BF16)] * heads, [VM] * 4 + [ANY] * heads,
        [pltpu.VMEM(g.shape, F32), pltpu.VMEM((heads, rows, N), BF16), pltpu.SemaphoreType.DMA((heads,))],
        3 << 30,
    )(place, g, near, far, k, p, y, t, o, see, run)


def delta_source(place, g, k, p, t, see, run, low, attended):
    heads, count = k.shape[:2]
    rows = count * C
    square, thin = (shaped((heads,) + tail) for tail in ((count, N, N), (count, C, N)))
    return single(
        functools.partial(source_kernel, heads, count), "delta_source",
        [SCALAR] + [VM] * 7 + [ANY] * heads,
        [thin, square, square, shaped((heads, N, N)), shaped(low.shape, BF16)], [VM] * 5,
        [pltpu.VMEM(g.shape, F32), pltpu.VMEM((heads, rows, N), BF16), pltpu.SemaphoreType.DMA((heads,))],
        3 << 30,
    )(place, g, k, p, t, see, run, low, *attended)


def delta_final(betas, decays, near, far, k, kt, inv, t, fade, col, s, u, dw, dq, q, z, b):
    heads, count = k.shape[:2]
    wide = (2 * count * C * heads, N)
    return single(
        functools.partial(final_kernel, heads, count), "delta_final",
        [VM] * 16,
        [shaped(wide, BF16), shaped(wide, BF16), shaped(betas.shape), shaped(decays.shape)], [VM] * 4,
        [pltpu.VMEM(wide, F32)] * 2 + [pltpu.VMEM((heads, count, N, N), F32)] * 4,
        8 << 30,
    )(decays, near, far, k, kt, inv, t, fade, col, s, u, dw, dq, q, z, b)


def rounds(refs, index, count, sign):
    return [lax.rem(index + (s if sign > 0 else count - s), count) for s in range(count)]


def send_kernel(count, place_ref, q_ref, k_ref, v_ref, *rest):
    outs, (low, scr, sem) = rest[:count], rest[count:]
    heads = count
    rows = q_ref.shape[0] // heads
    copies = [pltpu.make_async_copy(ref, low.at[m], sem.at[m]) for m, ref in enumerate((q_ref, k_ref, v_ref))]
    for copy in copies:
        copy.start()
    for m in range(3):
        copies[m].wait()
        scr[m] = low[m].astype(F32)
        for s in range(count):
            head = lax.rem(place_ref[0] + s, count)
            outs[s][m] = scr[m, pl.ds(head, rows, stride=heads), :].astype(BF16)


def take_kernel(count, place_ref, *rest):
    ins, outs, (scr,) = rest[:count], rest[count:count + 3], rest[count + 3:]
    heads = count
    rows = outs[0].shape[0] // heads
    for m in range(3):
        for s in range(count):
            head = lax.rem(place_ref[0] + count - s, count)
            scr[pl.ds(head, rows, stride=heads), :] = ins[s][m].astype(F32)
        outs[m][...] = scr[...].astype(BF16)


def attend_kernel(count, scale, place_ref, *rest):
    ins, (whole_ref, prob_ref, mixed_ref), outs = rest[:count], rest[count:count + 3], rest[count + 3:2 * count + 3]
    att_scr, sem = rest[2 * count + 3:]
    copies = gather_blocks(place_ref, ins, whole_ref, sem, 0)
    for copy in copies:
        copy.start()
    for copy in copies:
        copy.wait()
    rows = whole_ref.shape[2]
    causal = iota((rows, rows), 0) <= iota((rows, rows), 1)
    for i in range(count):
        query = whole_ref[i, 0]
        pieces = []
        for j in range(i + 1):
            score = contract(whole_ref[j, 1], query, 1, 1) * scale
            pieces.append(jnp.where(causal, score, -jnp.inf) if j == i else score)
        top = pieces[0].max(axis=0, keepdims=True)
        for piece in pieces[1:]:
            top = jnp.maximum(top, piece.max(axis=0, keepdims=True))
        pieces = [jnp.exp(piece - top) for piece in pieces]
        total = pieces[0].sum(axis=0, keepdims=True)
        for piece in pieces[1:]:
            total = total + piece.sum(axis=0, keepdims=True)
        share = 1.0 / total
        mixed = None
        for j, piece in enumerate(pieces):
            low = (piece * share).astype(BF16)
            prob_ref[i * (i + 1) // 2 + j] = low
            term = contract(low, whole_ref[j, 2], 0, 0)
            mixed = term if mixed is None else mixed + term
        mixed_ref[i] = mixed
        att_scr[i] = mixed.astype(BF16)
    copies = scatter_blocks(place_ref, att_scr, outs, sem, count)
    for copy in copies:
        copy.start()
    for copy in copies:
        copy.wait()


def attend_back_kernel(count, scale, place_ref, prob_ref, mixed_ref, whole_ref, *rest):
    grads, outs = rest[:count], rest[count:2 * count]
    g_scr, out_scr, acc, sem = rest[2 * count:]
    copies = gather_blocks(place_ref, grads, g_scr, sem, 0)
    for copy in copies:
        copy.start()
    for copy in copies:
        copy.wait()
    rows = whole_ref.shape[2]
    ones = jnp.ones((8, N), F32)
    for i in range(count - 1, -1, -1):
        mixed = mixed_ref[i]
        low = mixed.astype(BF16).astype(F32)
        grad = g_scr[i].astype(F32)
        inv = lax.rsqrt(jnp.mean(low * low, axis=1, keepdims=True) + EPS)
        pull = inv * (grad - low * (inv * inv * jnp.mean(low * grad, axis=1, keepdims=True)))
        pull = pull.astype(BF16)
        dots = mm_nt(ones, pull.astype(F32) * mixed)[:1]
        query = whole_ref[i, 0]
        gq = None
        for j in range(i + 1):
            prob = prob_ref[i * (i + 1) // 2 + j]
            gp = contract(whole_ref[j, 2], pull, 1, 1)
            gs = (prob.astype(F32) * (gp - dots) * scale).astype(BF16)
            term = contract(gs, whole_ref[j, 1], 0, 0)
            gq = term if gq is None else gq + term
            gk = contract(gs, query, 1, 0)
            gv = contract(prob, pull, 1, 0)
            if i < count - 1:
                gk, gv = gk + acc[j, 0], gv + acc[j, 1]
            if i == j:
                out_scr[j, 1] = gk.astype(BF16)
                out_scr[j, 2] = gv.astype(BF16)
            else:
                acc[j, 0] = gk
                acc[j, 1] = gv
        out_scr[i, 0] = gq.astype(BF16)
    copies = scatter_blocks(place_ref, out_scr, outs, sem, count)
    for copy in copies:
        copy.start()
    for copy in copies:
        copy.wait()


def send_heads(place, q, k, v, count):
    rows = q.shape[0] // count
    return single(
        functools.partial(send_kernel, count), "send_heads",
        [SCALAR, HBM, HBM, HBM], [shaped((3, rows, N), BF16)] * count, [VM] * count,
        [pltpu.VMEM((3,) + q.shape, BF16), pltpu.VMEM((3,) + q.shape, F32), pltpu.SemaphoreType.DMA((3,))],
        SENDFLOPS, SENDLIMIT,
    )(place, q, k, v)


def take_heads(place, parts):
    count = len(parts)
    rows = parts[0].shape[1]
    wide = (rows * count, N)
    return single(
        functools.partial(take_kernel, count), "take_heads",
        [SCALAR] + [VM] * count, [shaped(wide, BF16)] * 3, [VM] * 3,
        [pltpu.VMEM(wide, F32)], 1 << 28,
    )(place, *parts)


def attend(place, parts, scale):
    count = len(parts)
    rows = parts[0].shape[1]
    tri = count * (count + 1) // 2
    return single(
        functools.partial(attend_kernel, count, scale), "attend",
        [SCALAR] + [ANY] * count,
        [shaped((count, 3, rows, N), BF16), shaped((tri, rows, rows), BF16), shaped((count, rows, N))]
        + [shaped((rows, N), BF16)] * count,
        [VM] * 3 + [ANY] * count,
        [pltpu.VMEM((count, rows, N), BF16), pltpu.SemaphoreType.DMA((2 * count,))], 2 << 30,
    )(place, *parts)


def attend_back(place, prob, mixed, whole, grads, scale):
    count, _, rows, _ = whole.shape
    return single(
        functools.partial(attend_back_kernel, count, scale), "attend_back",
        [SCALAR, VM, VM, VM] + [ANY] * count,
        [shaped((3, rows, N), BF16)] * count, [ANY] * count,
        [pltpu.VMEM((count, rows, N), BF16), pltpu.VMEM((count, 3, rows, N), BF16),
         pltpu.VMEM((count, 2, rows, N), F32), pltpu.SemaphoreType.DMA((2 * count,))], 4 << 30,
    )(place, prob, mixed, whole, *grads)


PRECISE = lax.Precision.HIGHEST


def shifted(value, axis, steps):
    count = lax.axis_size(axis)
    initial, last = (max(0, -steps), min(count, count - steps))
    return lax.ppermute(value, axis, [(source, source + steps) for source in range(initial, last)])


def rotated(parts, axis):
    count = len(parts)
    moved = [parts[0]]
    for s in range(1, count):
        moved.append(lax.ppermute(parts[s], axis, [(d, (d + s) % count) for d in range(count)]))
    return moved


def apply_map(matrix, state):
    return jnp.einsum("hij,hjk->hik", matrix, state, precision=PRECISE)


def entering(low, matrix, offset, axis, step):
    count = lax.axis_size(axis)
    if count <= 4:
        near = shifted(low, axis, step)
        middle = (apply_map(matrix, near[0].astype(F32)) + offset).astype(BF16)
        return near, shifted(middle, axis, 2 * step), middle
    place = lax.axis_index(axis)
    place = place if step > 0 else count - 1 - place
    eye = jnp.eye(matrix.shape[-1], dtype=F32)
    reach = 1
    while reach < count:
        before, start = (shifted(matrix, axis, step * reach), shifted(offset, axis, step * reach))
        before = before + jnp.where(place < reach, eye, 0.0)
        offset = apply_map(matrix, start) + offset
        matrix = apply_map(matrix, before)
        reach *= 2
    state = shifted(offset, axis, step).astype(BF16)
    return jnp.stack([state, jnp.zeros_like(state)]), jnp.zeros_like(state), state


def visible_pairs(rows, span):
    relative = jnp.arange((span + 1) * rows, dtype=jnp.int32) - span * rows
    local = jnp.arange(rows, dtype=jnp.int32)
    return (
        (relative[None, :] <= local[:, None])
        & (relative[None, :] > local[:, None] - WINDOW)
        & (lax.axis_index("seq") * rows + relative[None, :] >= 0)
    )


def window_forward(queries, keys, values, scale):
    rows = queries.shape[0]
    span = -(-WINDOW // rows)
    couple = jnp.stack([keys, values])
    earlier = [shifted(couple, "seq", step + 1) for step in range(min(span, lax.axis_size("seq") - 1))]
    span = len(earlier)
    ordered = earlier[::-1] + [couple]
    window_keys = jnp.concatenate([piece[0] for piece in ordered], axis=0)
    window_values = jnp.concatenate([piece[1] for piece in ordered], axis=0)
    visible = visible_pairs(rows, span)
    scores = jnp.einsum("qhe,khe->hqk", queries, window_keys, preferred_element_type=F32) * scale
    top = jnp.max(jnp.where(visible, scores, -jnp.inf), axis=-1)
    lifted = jnp.where(visible, jnp.exp(jnp.where(visible, scores - top[:, :, None], 0.0)), 0.0)
    attention = lifted / jnp.sum(lifted, axis=-1)[:, :, None]
    mixed = jnp.einsum(
        "hqk,khe->qhe", attention.astype(BF16), window_values, preferred_element_type=F32
    )
    return window_keys, window_values, attention, mixed, span


def window_backward(queries, window_keys, window_values, attention, mixed, span, unit_grad, scale):
    rows = queries.shape[0]
    low = mixed.astype(BF16).astype(F32)
    grad = unit_grad.astype(F32)
    inv = lax.rsqrt(jnp.mean(low * low, axis=-1, keepdims=True) + EPS)
    pull = inv * (grad - low * (inv * inv * jnp.mean(low * grad, axis=-1, keepdims=True)))
    pull = pull.astype(BF16)
    row_dots = jnp.sum(pull.astype(F32) * mixed, axis=-1).T
    grad_attention = jnp.einsum("qhe,khe->hqk", pull, window_values, preferred_element_type=F32)
    grad_scores = (attention * (grad_attention - row_dots[:, :, None]) * scale).astype(BF16)
    grad_queries = jnp.einsum(
        "hqk,khe->qhe", grad_scores, window_keys, preferred_element_type=F32
    ).astype(BF16)
    key_parts = jnp.einsum("hqk,qhe->khe", grad_scores, queries, preferred_element_type=F32)
    value_parts = jnp.einsum("hqk,qhe->khe", attention.astype(BF16), pull, preferred_element_type=F32)
    gathered = jnp.stack([key_parts[span * rows:], value_parts[span * rows:]])
    for later in range(1, span + 1):
        first = (span - later) * rows
        piece = jnp.stack([key_parts[first:first + rows], value_parts[first:first + rows]])
        gathered = gathered + shifted(piece, "seq", -later)
    return grad_queries, gathered[0].astype(BF16), gathered[1].astype(BF16)


def body(queries, keys, values, delta_keys, delta_values, betas, decays, grad_out):
    rows, heads, width = queries.shape
    scale = 1.0 / math.sqrt(width)
    count = lax.axis_size("seq")
    by_head = heads == count and WINDOW >= count * rows

    def flat(array):
        return array.reshape(-1, width)

    place = lax.axis_index("seq").astype(jnp.int32).reshape(1) if by_head else jnp.zeros((1,), jnp.int32)
    extra = (flat(delta_keys), flat(delta_values), betas, decays)
    if by_head:
        parts = send_heads(place, flat(queries), flat(keys), flat(values), count)
        first, parts = lax.optimization_barrier((extra[0], parts))
        extra = (first,) + extra[1:]
        parts = rotated(parts, "seq")
    cot = flat(grad_out)
    k, kt, inverse, p, y, t, o, fade, see, run, col, shard_t, shard_o, low = delta_local(*extra)
    near, far, middle = entering(low, shard_t, shard_o, "seq", 1)
    if by_head:
        whole, prob, mixed, *attended = attend(place, parts, scale)
        attended = rotated(attended, "seq")
    else:
        saved = window_forward(queries, keys, values, scale)
        rounded = saved[3].astype(BF16)
        attended = [rounded[:, (heads - s) % heads] for s in range(heads)]
    s, u, dw, dq, *pulls = delta_readout(place, cot, near, far, k, p, y, t, o, see, run)
    if by_head:
        pulls = rotated(pulls, "seq")
        outs = rotated(attend_back(place, prob, mixed, whole, pulls, scale), "seq")
    else:
        grads = window_backward(queries, *saved, jnp.stack(pulls, axis=1), scale)
    attended, _ = lax.optimization_barrier((attended, middle))
    q, z, b, shard_source, low = delta_source(place, cot, k, p, t, see, run, low, attended)
    near, far, _ = entering(low, jnp.swapaxes(shard_t, 1, 2), shard_source, "seq", -1)
    grad_keys, grad_values, grad_betas, grad_decays = delta_final(
        betas, decays, near, far, k, kt, inverse, t, fade, col, s, u, dw, dq, q, z, b
    )
    if by_head:
        outs, grad_keys = lax.optimization_barrier((outs, grad_keys))
        grads = [array.reshape(rows, heads, width) for array in take_heads(place, outs)]
    pair = (rows, 2, heads, width)
    return (*grads, grad_keys.reshape(pair), grad_values.reshape(pair), grad_betas, grad_decays)


def solution(mesh):
    row = P(("parts", "seq"), "head", None)
    pair = P(("parts", "seq"), None, "head", None)
    beta = P(None, "head", ("parts", "seq"))
    decay = P("head", ("parts", "seq"))
    return jax.shard_map(
        body,
        mesh=mesh,
        in_specs=(row, row, row, pair, pair, beta, decay, row),
        out_specs=(row, row, row, pair, pair, beta, decay),
        check_vma=False,
    )
```

```python
import functools, math
import jax
import jax.numpy as jnp
from jax import lax
from jax.experimental import pallas as pl
from jax.experimental.pallas import tpu as pltpu
from jax.sharding import PartitionSpec as P

WINDOW = 1024

F32 = jnp.float32
BF16 = jnp.bfloat16
EPS = 1e-06
C = 64
N = 128
LIMIT = 16 * 1024 * 1024
SENDLIMIT = 58 * 1024 * 1024
SENDFLOPS = 20 << 30


def split(a):
    high = a.astype(BF16)
    return high, (a - high.astype(F32)).astype(BF16)


def contract(a, b, ca, cb):
    return lax.dot_general(a, b, (((ca,), (cb,)), ((), ())), preferred_element_type=F32)


def mm(a, b):
    ah, al = split(a)
    bh, bl = split(b)
    wide = jnp.concatenate([bh, bl], axis=1)
    both = contract(jnp.concatenate([ah, al], axis=1), jnp.concatenate([wide, wide], axis=0), 1, 0)
    half = b.shape[1]
    return both[:, :half] + both[:, half:]


def mm_nt(a, b):
    ah, al = split(a)
    bh, bl = split(b)
    tall = jnp.concatenate([bh, bl], axis=0)
    both = contract(jnp.concatenate([ah, al], axis=1), jnp.concatenate([tall, tall], axis=1), 1, 1)
    half = b.shape[0]
    return both[:, :half] + both[:, half:]


def mm_tn(a, b):
    ah, al = split(a)
    bh, bl = split(b)
    wide = jnp.concatenate([bh, bl], axis=1)
    both = contract(jnp.concatenate([ah, al], axis=0), jnp.concatenate([wide, wide], axis=0), 0, 0)
    half = b.shape[1]
    return both[:, :half] + both[:, half:]


def low_nt(low, b):
    bh, bl = split(b)
    both = contract(low, jnp.concatenate([bh, bl], axis=0), 1, 1)
    half = b.shape[0]
    return both[:, :half] + both[:, half:]


def low_tn(a, low):
    ah, al = split(a)
    return contract(jnp.concatenate([ah, al], axis=0), jnp.concatenate([low, low], axis=0), 0, 0)


def iota(shape, axis):
    return lax.broadcasted_iota(jnp.int32, shape, axis)


class Grid:
    def __init__(self):
        self.row = iota((N, N), 0)
        self.lane = iota((N, N), 1)
        self.row_pos = self.row & (C - 1)
        self.lane_pos = self.lane & (C - 1)
        key_row = 2 * self.row_pos + (self.row >> 6)
        key_lane = 2 * self.lane_pos + (self.lane >> 6)
        self.strict = key_row > key_lane
        self.differ = key_row ^ key_lane
        self.diag = self.row == self.lane

    def to_row(self, column):
        return jnp.sum(jnp.where(self.diag, column, 0.0), axis=0, keepdims=True)

    def to_column(self, line):
        return jnp.sum(jnp.where(self.diag, line, 0.0), axis=1, keepdims=True)


def gates(grid, betas_ref, decays_ref, h, c):
    pair, half = c // 2, C * (c % 2)
    lanes = pl.ds(pair * N, N)
    first = betas_ref[0, pl.ds(h, 1), lanes]
    second = betas_ref[1, pl.ds(h, 1), lanes]
    logs = jnp.log(decays_ref[pl.ds(h, 1), lanes])
    offset = grid.lane - half
    chosen = jnp.where(grid.row < C, first, second)
    beta = jnp.sum(jnp.where(offset == grid.row_pos, chosen, 0.0), axis=1, keepdims=True)
    seen = (offset >= 0) & (offset <= grid.row_pos)
    run = jnp.sum(jnp.where(seen, logs, 0.0), axis=1, keepdims=True)
    inside = (offset[:1] >= 0) & (offset[:1] < C)
    end = jnp.sum(jnp.where(inside, logs, 0.0), axis=1, keepdims=True)
    return beta, run, grid.to_row(run), end


def pair_rows(ref, heads, h, c):
    base = c * C * 2 * heads
    return jnp.concatenate(
        [
            ref[pl.ds(base + h, C, stride=2 * heads), :],
            ref[pl.ds(base + heads + h, C, stride=2 * heads), :],
        ],
        axis=0,
    )


BETA, READ, TAIL, SCALE = range(4)


def pair_product(ah, al, bh, bl):
    wide = jnp.concatenate([bh, bl], axis=1)
    both = contract(jnp.concatenate([ah, al], axis=1), jnp.concatenate([wide, wide], axis=0), 1, 0)
    half = bh.shape[1]
    return both[:, :half] + both[:, half:]


def local_kernel(heads, count, dk_ref, dv_ref, betas_ref, decays_ref,
                 k_ref, kt_ref, inv_ref, p_ref, y_ref, t_ref, o_ref, fade_ref, see_ref, run_ref, col_ref,
                 tsh_ref, osh_ref, low_ref,
                 keys_scr, values_scr, sys_scr, split_scr, half_scr, rhs_scr):
    grid = Grid()
    eye = jnp.where(grid.diag, 1.0, 0.0)
    items = [(h, c) for h in range(heads) for c in range(count)]
    keys_scr[...] = dk_ref[...].astype(F32)
    values_scr[...] = dv_ref[...].astype(F32)
    ends = {}
    for h, c in items:
        raw = pair_rows(keys_scr, heads, h, c)
        values = pair_rows(values_scr, heads, h, c)
        scale = lax.rsqrt(jnp.sum(raw * raw, axis=1, keepdims=True) + EPS)
        keys = raw * scale
        beta, run, line, end = gates(grid, betas_ref, decays_ref, h, c)
        tail = jnp.exp(end - run)
        read = beta * jnp.exp(run)
        fade = beta * jnp.where(grid.strict, jnp.exp(jnp.minimum(run - line, 0.0)), 0.0)
        seen = grid.lane_pos[:C] <= grid.row_pos[:C]
        see_ref[h, c] = jnp.where(seen, jnp.exp(jnp.minimum(run[:C] - line, 0.0)), 0.0)
        run_ref[h, c] = jnp.broadcast_to(jnp.exp(run[:C]), (C, N))
        col_ref[h, c] = jnp.where(
            grid.lane == BETA, beta,
            jnp.where(grid.lane == READ, read, jnp.where(grid.lane == TAIL, tail, scale)),
        )
        k_ref[h, c] = keys
        kt_ref[h, c] = keys * tail
        fade_ref[h, c] = fade
        system = fade * mm_nt(keys, keys)
        sys_scr[0, h, c], sys_scr[1, h, c] = split(system)
        inverse = eye - jnp.where(grid.differ == 1, system, 0.0)
        inv_ref[h, c] = inverse
        split_scr[0, h, c], split_scr[1, h, c] = split(inverse)
        rhs_scr[h, c, :, :N] = read * keys
        rhs_scr[h, c, :, N:] = beta * values
        ends[h, c] = jnp.exp(end)
    for level in range(1, 7):
        near = (grid.differ >= (1 << level)) & (grid.differ < (2 << level))
        near = jnp.where(near, 1.0, 0.0).astype(BF16)
        for h, c in items:
            half = pair_product(
                sys_scr[0, h, c] * near, sys_scr[1, h, c] * near, split_scr[0, h, c], split_scr[1, h, c]
            )
            half_scr[0, h, c], half_scr[1, h, c] = split(half)
        for h, c in items:
            inverse = inv_ref[h, c] - pair_product(
                split_scr[0, h, c], split_scr[1, h, c], half_scr[0, h, c], half_scr[1, h, c]
            )
            inv_ref[h, c] = inverse
            split_scr[0, h, c], split_scr[1, h, c] = split(inverse)
    for h, c in items:
        both = pair_product(split_scr[0, h, c], split_scr[1, h, c], *split(rhs_scr[h, c]))
        p_ref[h, c] = both[:, :N]
        y_ref[h, c] = both[:, N:]
    for i in items:
        maps = mm_tn(kt_ref[i], jnp.concatenate([p_ref[i], y_ref[i]], axis=1))
        t_ref[i] = ends[i] * eye - maps[:, :N]
        o_ref[i] = maps[:, N:]
    for h in range(heads):
        tsh_ref[h] = t_ref[h, 0]
        osh_ref[h] = o_ref[h, 0]
    for c in range(1, count):
        for h in range(heads):
            both = mm(t_ref[h, c], jnp.concatenate([tsh_ref[h], osh_ref[h]], axis=1))
            tsh_ref[h] = both[:, :N]
            osh_ref[h] = both[:, N:] + o_ref[h, c]
    for h in range(heads):
        low_ref[0, h] = osh_ref[h].astype(BF16)
        low_ref[1, h] = tsh_ref[h].astype(BF16)


def gather_blocks(place_ref, refs, scr):
    count = len(refs)
    for s in range(count):
        scr[lax.rem(place_ref[0] + count - s, count)] = refs[s][...]


def scatter_blocks(place_ref, scr, refs):
    count = len(refs)
    for s in range(count):
        refs[s][...] = scr[lax.rem(place_ref[0] + s, count)]


def head_rows(ref, heads, h, c):
    return ref[pl.ds(c * C * heads + h, C, stride=heads), :]


def readout_kernel(heads, count, place_ref, g_ref, near_ref, far_ref, k_ref, p_ref, y_ref, t_ref, o_ref, see_ref, run_ref,
                   s_ref, u_ref, dw_ref, dq_ref, *rest):
    outs, (g_scr, dq_scr) = rest[:heads], rest[heads:]
    g_scr[...] = g_ref[...].astype(F32)
    for h in range(heads):
        s_ref[h, 0] = near_ref[0, h].astype(F32) + contract(near_ref[1, h], far_ref[h], 1, 0)
    for c in range(count):
        for h in range(heads):
            both = mm(jnp.concatenate([t_ref[h, c], p_ref[h, c]], axis=0), s_ref[h, c])
            u_ref[h, c] = y_ref[h, c] - both[N:]
            s_ref[h, c + 1] = both[:N] + o_ref[h, c]
    items = [(h, c) for h in range(heads) for c in range(count)]
    for h, c in items:
        cot = head_rows(g_scr, heads, h, c).astype(BF16)
        both = low_nt(cot, jnp.concatenate([u_ref[h, c], s_ref[h, c]], axis=0))
        dw_ref[h, c] = both[:, :N] * see_ref[h, c]
        dq_ref[h, c] = run_ref[h, c] * both[:, N:]
    for h, c in items:
        grad = mm(dw_ref[h, c], k_ref[h, c]) + dq_ref[h, c]
        dq_ref[h, c] = grad
        dq_scr[h, pl.ds(c * C, C), :] = grad.astype(BF16)
    scatter_blocks(place_ref, dq_scr, outs)


def unit_queries(low):
    raw = low.astype(F32)
    return raw * lax.rsqrt(jnp.mean(raw * raw, axis=1, keepdims=True) + EPS)


def source_kernel(heads, count, place_ref, g_ref, k_ref, p_ref, t_ref, see_ref, run_ref, map_ref, *rest):
    ins, (q_ref, z_ref, b_ref, bsh_ref, low_ref, g_scr, q_scr) = rest[:heads], rest[heads:]
    gather_blocks(place_ref, ins, q_scr)
    g_scr[...] = g_ref[...].astype(F32)
    items = [(h, c) for h in range(heads) for c in range(count)]
    weights = {}
    for h, c in items:
        query = unit_queries(q_scr[h, pl.ds(c * C, C), :])
        q_ref[h, c] = query
        weights[h, c] = mm_nt(query, k_ref[h, c]) * see_ref[h, c]
    for h, c in items:
        cot = head_rows(g_scr, heads, h, c).astype(BF16)
        z_ref[h, c] = low_tn(weights[h, c], cot)
        b_ref[h, c] = low_tn(q_ref[h, c] * run_ref[h, c], cot)
    for h, c in items:
        b_ref[h, c] = b_ref[h, c] - mm_tn(p_ref[h, c], z_ref[h, c])
    for h in range(heads):
        bsh_ref[h] = b_ref[h, count - 1]
    for c in range(count - 2, -1, -1):
        for h in range(heads):
            bsh_ref[h] = b_ref[h, c] + mm_tn(t_ref[h, c], bsh_ref[h])
    for h in range(heads):
        low_ref[0, h] = bsh_ref[h].astype(BF16)
        low_ref[1, h] = map_ref[1, h]


def final_kernel(heads, count, decays_ref, near_ref, far_ref, k_ref, kt_ref, inv_ref, t_ref, fade_ref, col_ref,
                 s_ref, u_ref, dw_ref, dq_ref, q_ref, z_ref, b_ref,
                 gk_ref, gv_ref, gb_ref, gd_ref, gk_scr, gv_scr, lam_scr, r_scr, d_scr, rd_scr):
    grid = Grid()
    items = [(h, c) for h in range(heads) for c in range(count)]
    for h in range(heads):
        lam_scr[h, count - 1] = near_ref[0, h].astype(F32) + contract(near_ref[1, h], far_ref[h], 0, 0)
    for c in range(count - 1, 0, -1):
        for h in range(heads):
            lam_scr[h, c - 1] = mm_tn(t_ref[h, c], lam_scr[h, c]) + b_ref[h, c]
    for i in items:
        d_scr[i] = z_ref[i] + mm(kt_ref[i], lam_scr[i])
    for i in items:
        r_scr[i] = mm_tn(inv_ref[i], d_scr[i])
    for h, c in items:
        both = mm_nt(r_scr[h, c], jnp.concatenate([u_ref[h, c], s_ref[h, c]], axis=0))
        d_scr[h, c] = -both[:, :N] * fade_ref[h, c]
        rd_scr[h, c] = -col_ref[h, c, :, READ:READ + 1] * both[:, N:]
    lines = {}
    for h, c in items:
        keys, r = k_ref[h, c], r_scr[h, c]
        cols = col_ref[h, c]
        beta, tail, scale = (cols[:, n:n + 1] for n in (BETA, TAIL, SCALE))
        gb = jnp.sum(r * u_ref[h, c], axis=1, keepdims=True) / beta
        read = mm(d_scr[h, c], keys) + rd_scr[h, c]
        query = q_ref[h, c]
        write = mm_tn(d_scr[h, c], keys) + tail * mm_nt(u_ref[h, c], lam_scr[h, c]) + mm_tn(dw_ref[h, c], query)
        grad = read + write
        gk = scale * (grad - keys * jnp.sum(keys * grad, axis=1, keepdims=True))
        gv = beta * r
        base = c * C * 2 * heads
        for m in range(2):
            rows = pl.ds(base + m * heads + h, C, stride=2 * heads)
            gk_scr[rows, :] = gk[m * C:(m + 1) * C]
            gv_scr[rows, :] = gv[m * C:(m + 1) * C]
        pulls = keys * (read - write)
        pulls = jnp.sum(pulls[:C] + pulls[C:] + query * dq_ref[h, c], axis=1, keepdims=True)
        after = grid.row_pos[:C] >= grid.lane_pos[:C]
        total = jnp.sum(
            jnp.sum(s_ref[h, c + 1] * lam_scr[h, c], axis=0, keepdims=True), axis=1, keepdims=True
        )
        gd = jnp.sum(jnp.where(after, pulls, 0.0), axis=0, keepdims=True) + total
        half = C * (c % 2)
        mine = (grid.lane[:1] >= half) & (grid.lane[:1] < half + C)
        lines[h, c, 2] = jnp.where(mine, gd, 0.0)
        for m in range(2):
            pick = (grid.lane - half == grid.row - m * C) & (grid.row >= m * C) & (grid.row < (m + 1) * C)
            lines[h, c, m] = jnp.sum(jnp.where(pick, gb, 0.0), axis=0, keepdims=True)
    for h in range(heads):
        for p in range(count // 2):
            lanes = pl.ds(p * N, N)
            for m in range(2):
                gb_ref[m, pl.ds(h, 1), lanes] = lines[h, 2 * p, m] + lines[h, 2 * p + 1, m]
            gd_ref[pl.ds(h, 1), lanes] = (lines[h, 2 * p, 2] + lines[h, 2 * p + 1, 2]) / decays_ref[pl.ds(h, 1), lanes]
    gk_ref[...] = gk_scr[...].astype(BF16)
    gv_ref[...] = gv_scr[...].astype(BF16)


HBM = pl.BlockSpec(memory_space=pltpu.HBM)
SCALAR = pl.BlockSpec(memory_space=pltpu.SMEM)
VM = pl.BlockSpec(memory_space=pltpu.VMEM)


def shaped(shape, dtype=F32):
    return jax.ShapeDtypeStruct(shape, dtype)


def single(body, name, in_specs, outs, out_specs, scratch, flops, limit=LIMIT):
    return pl.pallas_call(
        body,
        name=name,
        in_specs=in_specs,
        out_shape=outs,
        out_specs=out_specs,
        scratch_shapes=scratch,
        compiler_params=pltpu.CompilerParams(vmem_limit_bytes=limit),
        cost_estimate=pl.CostEstimate(flops=flops, bytes_accessed=4 << 20, transcendentals=0),
    )


def delta_local(dk, dv, betas, decays):
    heads, rows = decays.shape
    count = rows // C
    square, thin, one = (shaped((heads,) + tail) for tail in ((count, N, N), (count, C, N), (N, N)))
    outs = [square] * 8 + [thin] * 2 + [square] + [one] * 2 + [shaped((2, heads, N, N), BF16)]
    halves = pltpu.VMEM((2, heads, count, N, N), BF16)
    return single(
        functools.partial(local_kernel, heads, count), "delta_local",
        [VM] * 4, outs, [VM] * len(outs),
        [pltpu.VMEM(dk.shape, F32)] * 2 + [halves] * 3
        + [pltpu.VMEM((heads, count, N, 2 * N), F32)],
        10 << 30,
    )(dk, dv, betas, decays)


def delta_readout(place, g, near, far, k, p, y, t, o, see, run):
    heads, count = k.shape[:2]
    rows = count * C
    square, thin = (shaped((heads,) + tail) for tail in ((count, N, N), (count, C, N)))
    outs = [shaped((heads, count + 1, N, N)), square, thin, thin]
    return single(
        functools.partial(readout_kernel, heads, count), "delta_readout",
        [SCALAR] + [VM] * 10, outs + [shaped((rows, N), BF16)] * heads, [VM] * (4 + heads),
        [pltpu.VMEM(g.shape, F32), pltpu.VMEM((heads, rows, N), BF16)],
        3 << 30,
    )(place, g, near, far, k, p, y, t, o, see, run)


def delta_source(place, g, k, p, t, see, run, low, attended):
    heads, count = k.shape[:2]
    rows = count * C
    square, thin = (shaped((heads,) + tail) for tail in ((count, N, N), (count, C, N)))
    return single(
        functools.partial(source_kernel, heads, count), "delta_source",
        [SCALAR] + [VM] * (7 + heads),
        [thin, square, square, shaped((heads, N, N)), shaped(low.shape, BF16)], [VM] * 5,
        [pltpu.VMEM(g.shape, F32), pltpu.VMEM((heads, rows, N), BF16)],
        3 << 30,
    )(place, g, k, p, t, see, run, low, *attended)


def delta_final(betas, decays, near, far, k, kt, inv, t, fade, col, s, u, dw, dq, q, z, b):
    heads, count = k.shape[:2]
    wide = (2 * count * C * heads, N)
    return single(
        functools.partial(final_kernel, heads, count), "delta_final",
        [VM] * 16,
        [shaped(wide, BF16), shaped(wide, BF16), shaped(betas.shape), shaped(decays.shape)], [VM] * 4,
        [pltpu.VMEM(wide, F32)] * 2 + [pltpu.VMEM((heads, count, N, N), F32)] * 4,
        8 << 30,
    )(decays, near, far, k, kt, inv, t, fade, col, s, u, dw, dq, q, z, b)


def rounds(refs, index, count, sign):
    return [lax.rem(index + (s if sign > 0 else count - s), count) for s in range(count)]


def send_kernel(count, place_ref, q_ref, k_ref, v_ref, *rest):
    outs, (low, scr, sem) = rest[:count], rest[count:]
    heads = count
    rows = q_ref.shape[0] // heads
    copies = [pltpu.make_async_copy(ref, low.at[m], sem.at[m]) for m, ref in enumerate((q_ref, k_ref, v_ref))]
    for copy in copies:
        copy.start()
    for m in range(3):
        copies[m].wait()
        scr[m] = low[m].astype(F32)
        for s in range(count):
            head = lax.rem(place_ref[0] + s, count)
            outs[s][m] = scr[m, pl.ds(head, rows, stride=heads), :].astype(BF16)


def take_kernel(count, place_ref, *rest):
    ins, outs, (scr,) = rest[:count], rest[count:count + 3], rest[count + 3:]
    heads = count
    rows = outs[0].shape[0] // heads
    for m in range(3):
        for s in range(count):
            head = lax.rem(place_ref[0] + count - s, count)
            scr[pl.ds(head, rows, stride=heads), :] = ins[s][m].astype(F32)
        outs[m][...] = scr[...].astype(BF16)


def attend_kernel(count, scale, place_ref, *rest):
    ins, (whole_ref, prob_ref, mixed_ref), outs = rest[:count], rest[count:count + 3], rest[count + 3:2 * count + 3]
    (att_scr,) = rest[2 * count + 3:]
    gather_blocks(place_ref, ins, whole_ref)
    rows = whole_ref.shape[2]
    causal = iota((rows, rows), 0) <= iota((rows, rows), 1)
    for i in range(count):
        query = whole_ref[i, 0]
        pieces = []
        for j in range(i + 1):
            score = contract(whole_ref[j, 1], query, 1, 1) * scale
            pieces.append(jnp.where(causal, score, -jnp.inf) if j == i else score)
        top = pieces[0].max(axis=0, keepdims=True)
        for piece in pieces[1:]:
            top = jnp.maximum(top, piece.max(axis=0, keepdims=True))
        pieces = [jnp.exp(piece - top) for piece in pieces]
        total = pieces[0].sum(axis=0, keepdims=True)
        for piece in pieces[1:]:
            total = total + piece.sum(axis=0, keepdims=True)
        share = 1.0 / total
        mixed = None
        for j, piece in enumerate(pieces):
            low = (piece * share).astype(BF16)
            prob_ref[i * (i + 1) // 2 + j] = low
            term = contract(low, whole_ref[j, 2], 0, 0)
            mixed = term if mixed is None else mixed + term
        mixed_ref[i] = mixed
        att_scr[i] = mixed.astype(BF16)
    scatter_blocks(place_ref, att_scr, outs)


def attend_back_kernel(count, scale, place_ref, prob_ref, mixed_ref, whole_ref, *rest):
    grads, outs = rest[:count], rest[count:2 * count]
    g_scr, out_scr, acc = rest[2 * count:]
    gather_blocks(place_ref, grads, g_scr)
    rows = whole_ref.shape[2]
    ones = jnp.ones((8, N), F32)
    for i in range(count - 1, -1, -1):
        mixed = mixed_ref[i]
        low = mixed.astype(BF16).astype(F32)
        grad = g_scr[i].astype(F32)
        inv = lax.rsqrt(jnp.mean(low * low, axis=1, keepdims=True) + EPS)
        pull = inv * (grad - low * (inv * inv * jnp.mean(low * grad, axis=1, keepdims=True)))
        pull = pull.astype(BF16)
        dots = mm_nt(ones, pull.astype(F32) * mixed)[:1]
        query = whole_ref[i, 0]
        gq = None
        for j in range(i + 1):
            prob = prob_ref[i * (i + 1) // 2 + j]
            gp = contract(whole_ref[j, 2], pull, 1, 1)
            gs = (prob.astype(F32) * (gp - dots) * scale).astype(BF16)
            term = contract(gs, whole_ref[j, 1], 0, 0)
            gq = term if gq is None else gq + term
            gk = contract(gs, query, 1, 0)
            gv = contract(prob, pull, 1, 0)
            if i < count - 1:
                gk, gv = gk + acc[j, 0], gv + acc[j, 1]
            if i == j:
                out_scr[j, 1] = gk.astype(BF16)
                out_scr[j, 2] = gv.astype(BF16)
            else:
                acc[j, 0] = gk
                acc[j, 1] = gv
        out_scr[i, 0] = gq.astype(BF16)
    scatter_blocks(place_ref, out_scr, outs)


def send_heads(place, q, k, v, count):
    rows = q.shape[0] // count
    return single(
        functools.partial(send_kernel, count), "send_heads",
        [SCALAR, HBM, HBM, HBM], [shaped((3, rows, N), BF16)] * count, [VM] * count,
        [pltpu.VMEM((3,) + q.shape, BF16), pltpu.VMEM((3,) + q.shape, F32), pltpu.SemaphoreType.DMA((3,))],
        SENDFLOPS, SENDLIMIT,
    )(place, q, k, v)


def take_heads(place, parts):
    count = len(parts)
    rows = parts[0].shape[1]
    wide = (rows * count, N)
    return single(
        functools.partial(take_kernel, count), "take_heads",
        [SCALAR] + [VM] * count, [shaped(wide, BF16)] * 3, [VM] * 3,
        [pltpu.VMEM(wide, F32)], 1 << 28,
    )(place, *parts)


def attend(place, parts, scale):
    count = len(parts)
    rows = parts[0].shape[1]
    tri = count * (count + 1) // 2
    return single(
        functools.partial(attend_kernel, count, scale), "attend",
        [SCALAR] + [VM] * count,
        [shaped((count, 3, rows, N), BF16), shaped((tri, rows, rows), BF16), shaped((count, rows, N))]
        + [shaped((rows, N), BF16)] * count,
        [VM] * (3 + count),
        [pltpu.VMEM((count, rows, N), BF16)], 2 << 30,
    )(place, *parts)


def attend_back(place, prob, mixed, whole, grads, scale):
    count, _, rows, _ = whole.shape
    return single(
        functools.partial(attend_back_kernel, count, scale), "attend_back",
        [SCALAR] + [VM] * (3 + count),
        [shaped((3, rows, N), BF16)] * count, [VM] * count,
        [pltpu.VMEM((count, rows, N), BF16), pltpu.VMEM((count, 3, rows, N), BF16),
         pltpu.VMEM((count, 2, rows, N), F32)], 4 << 30,
    )(place, prob, mixed, whole, *grads)


PRECISE = lax.Precision.HIGHEST


def shifted(value, axis, steps):
    count = lax.axis_size(axis)
    initial, last = (max(0, -steps), min(count, count - steps))
    return lax.ppermute(value, axis, [(source, source + steps) for source in range(initial, last)])


def rotated(parts, axis):
    count = len(parts)
    moved = [parts[0]]
    for s in range(1, count):
        moved.append(lax.ppermute(parts[s], axis, [(d, (d + s) % count) for d in range(count)]))
    return moved


def apply_map(matrix, state):
    return jnp.einsum("hij,hjk->hik", matrix, state, precision=PRECISE)


def entering(low, matrix, offset, axis, step):
    count = lax.axis_size(axis)
    if count <= 4:
        near = shifted(low, axis, step)
        middle = (apply_map(matrix, near[0].astype(F32)) + offset).astype(BF16)
        return near, shifted(middle, axis, 2 * step), middle
    place = lax.axis_index(axis)
    place = place if step > 0 else count - 1 - place
    eye = jnp.eye(matrix.shape[-1], dtype=F32)
    reach = 1
    while reach < count:
        before, start = (shifted(matrix, axis, step * reach), shifted(offset, axis, step * reach))
        before = before + jnp.where(place < reach, eye, 0.0)
        offset = apply_map(matrix, start) + offset
        matrix = apply_map(matrix, before)
        reach *= 2
    state = shifted(offset, axis, step).astype(BF16)
    return jnp.stack([state, jnp.zeros_like(state)]), jnp.zeros_like(state), state


def visible_pairs(rows, span):
    relative = jnp.arange((span + 1) * rows, dtype=jnp.int32) - span * rows
    local = jnp.arange(rows, dtype=jnp.int32)
    return (
        (relative[None, :] <= local[:, None])
        & (relative[None, :] > local[:, None] - WINDOW)
        & (lax.axis_index("seq") * rows + relative[None, :] >= 0)
    )


def window_forward(queries, keys, values, scale):
    rows = queries.shape[0]
    span = -(-WINDOW // rows)
    couple = jnp.stack([keys, values])
    earlier = [shifted(couple, "seq", step + 1) for step in range(min(span, lax.axis_size("seq") - 1))]
    span = len(earlier)
    ordered = earlier[::-1] + [couple]
    window_keys = jnp.concatenate([piece[0] for piece in ordered], axis=0)
    window_values = jnp.concatenate([piece[1] for piece in ordered], axis=0)
    visible = visible_pairs(rows, span)
    scores = jnp.einsum("qhe,khe->hqk", queries, window_keys, preferred_element_type=F32) * scale
    top = jnp.max(jnp.where(visible, scores, -jnp.inf), axis=-1)
    lifted = jnp.where(visible, jnp.exp(jnp.where(visible, scores - top[:, :, None], 0.0)), 0.0)
    attention = lifted / jnp.sum(lifted, axis=-1)[:, :, None]
    mixed = jnp.einsum(
        "hqk,khe->qhe", attention.astype(BF16), window_values, preferred_element_type=F32
    )
    return window_keys, window_values, attention, mixed, span


def window_backward(queries, window_keys, window_values, attention, mixed, span, unit_grad, scale):
    rows = queries.shape[0]
    low = mixed.astype(BF16).astype(F32)
    grad = unit_grad.astype(F32)
    inv = lax.rsqrt(jnp.mean(low * low, axis=-1, keepdims=True) + EPS)
    pull = inv * (grad - low * (inv * inv * jnp.mean(low * grad, axis=-1, keepdims=True)))
    pull = pull.astype(BF16)
    row_dots = jnp.sum(pull.astype(F32) * mixed, axis=-1).T
    grad_attention = jnp.einsum("qhe,khe->hqk", pull, window_values, preferred_element_type=F32)
    grad_scores = (attention * (grad_attention - row_dots[:, :, None]) * scale).astype(BF16)
    grad_queries = jnp.einsum(
        "hqk,khe->qhe", grad_scores, window_keys, preferred_element_type=F32
    ).astype(BF16)
    key_parts = jnp.einsum("hqk,qhe->khe", grad_scores, queries, preferred_element_type=F32)
    value_parts = jnp.einsum("hqk,qhe->khe", attention.astype(BF16), pull, preferred_element_type=F32)
    gathered = jnp.stack([key_parts[span * rows:], value_parts[span * rows:]])
    for later in range(1, span + 1):
        first = (span - later) * rows
        piece = jnp.stack([key_parts[first:first + rows], value_parts[first:first + rows]])
        gathered = gathered + shifted(piece, "seq", -later)
    return grad_queries, gathered[0].astype(BF16), gathered[1].astype(BF16)


def body(queries, keys, values, delta_keys, delta_values, betas, decays, grad_out):
    rows, heads, width = queries.shape
    scale = 1.0 / math.sqrt(width)
    count = lax.axis_size("seq")
    by_head = heads == count and WINDOW >= count * rows

    def flat(array):
        return array.reshape(-1, width)

    place = lax.axis_index("seq").astype(jnp.int32).reshape(1) if by_head else jnp.zeros((1,), jnp.int32)
    extra = (flat(delta_keys), flat(delta_values), betas, decays)
    if by_head:
        parts = send_heads(place, flat(queries), flat(keys), flat(values), count)
        first, parts = lax.optimization_barrier((extra[0], parts))
        extra = (first,) + extra[1:]
        parts = rotated(parts, "seq")
    cot = flat(grad_out)
    k, kt, inverse, p, y, t, o, fade, see, run, col, shard_t, shard_o, low = delta_local(*extra)
    near, far, middle = entering(low, shard_t, shard_o, "seq", 1)
    if by_head:
        whole, prob, mixed, *attended = attend(place, parts, scale)
        attended = rotated(attended, "seq")
    else:
        saved = window_forward(queries, keys, values, scale)
        rounded = saved[3].astype(BF16)
        attended = [rounded[:, (heads - s) % heads] for s in range(heads)]
    s, u, dw, dq, *pulls = delta_readout(place, cot, near, far, k, p, y, t, o, see, run)
    if by_head:
        pulls = rotated(pulls, "seq")
        outs = rotated(attend_back(place, prob, mixed, whole, pulls, scale), "seq")
    else:
        grads = window_backward(queries, *saved, jnp.stack(pulls, axis=1), scale)
    attended, _ = lax.optimization_barrier((attended, middle))
    q, z, b, shard_source, low = delta_source(place, cot, k, p, t, see, run, low, attended)
    near, far, _ = entering(low, jnp.swapaxes(shard_t, 1, 2), shard_source, "seq", -1)
    grad_keys, grad_values, grad_betas, grad_decays = delta_final(
        betas, decays, near, far, k, kt, inverse, t, fade, col, s, u, dw, dq, q, z, b
    )
    if by_head:
        outs, grad_keys = lax.optimization_barrier((outs, grad_keys))
        grads = [array.reshape(rows, heads, width) for array in take_heads(place, outs)]
    pair = (rows, 2, heads, width)
    return (*grads, grad_keys.reshape(pair), grad_values.reshape(pair), grad_betas, grad_decays)


def solution(mesh):
    row = P(("parts", "seq"), "head", None)
    pair = P(("parts", "seq"), None, "head", None)
    beta = P(None, "head", ("parts", "seq"))
    decay = P("head", ("parts", "seq"))
    return jax.shard_map(
        body,
        mesh=mesh,
        in_specs=(row, row, row, pair, pair, beta, decay, row),
        out_specs=(row, row, row, pair, pair, beta, decay),
        check_vma=False,
    )
```

```python
import functools, math
import jax
import jax.numpy as jnp
from jax import lax
from jax.experimental import pallas as pl
from jax.experimental.pallas import tpu as pltpu
from jax.sharding import PartitionSpec as P

WINDOW = 1024

F32 = jnp.float32
BF16 = jnp.bfloat16
EPS = 1e-06
C = 64
N = 128
LIMIT = 16 * 1024 * 1024
SENDLIMIT = 58 * 1024 * 1024
SENDFLOPS = 20 << 30


def split(a):
    high = a.astype(BF16)
    return high, (a - high.astype(F32)).astype(BF16)


def contract(a, b, ca, cb):
    return lax.dot_general(a, b, (((ca,), (cb,)), ((), ())), preferred_element_type=F32)


def mm(a, b):
    ah, al = split(a)
    bh, bl = split(b)
    wide = jnp.concatenate([bh, bl], axis=1)
    both = contract(jnp.concatenate([ah, al], axis=1), jnp.concatenate([wide, wide], axis=0), 1, 0)
    half = b.shape[1]
    return both[:, :half] + both[:, half:]


def mm_nt(a, b):
    ah, al = split(a)
    bh, bl = split(b)
    tall = jnp.concatenate([bh, bl], axis=0)
    both = contract(jnp.concatenate([ah, al], axis=1), jnp.concatenate([tall, tall], axis=1), 1, 1)
    half = b.shape[0]
    return both[:, :half] + both[:, half:]


def mm_tn(a, b):
    ah, al = split(a)
    bh, bl = split(b)
    wide = jnp.concatenate([bh, bl], axis=1)
    both = contract(jnp.concatenate([ah, al], axis=0), jnp.concatenate([wide, wide], axis=0), 0, 0)
    half = b.shape[1]
    return both[:, :half] + both[:, half:]


def low_nt(low, b):
    bh, bl = split(b)
    both = contract(low, jnp.concatenate([bh, bl], axis=0), 1, 1)
    half = b.shape[0]
    return both[:, :half] + both[:, half:]


def low_tn(a, low):
    ah, al = split(a)
    return contract(jnp.concatenate([ah, al], axis=0), jnp.concatenate([low, low], axis=0), 0, 0)


def iota(shape, axis):
    return lax.broadcasted_iota(jnp.int32, shape, axis)


class Grid:
    def __init__(self):
        self.row = iota((N, N), 0)
        self.lane = iota((N, N), 1)
        self.row_pos = self.row & (C - 1)
        self.lane_pos = self.lane & (C - 1)
        key_row = 2 * self.row_pos + (self.row >> 6)
        key_lane = 2 * self.lane_pos + (self.lane >> 6)
        self.strict = key_row > key_lane
        self.differ = key_row ^ key_lane
        self.diag = self.row == self.lane

    def to_row(self, column):
        return jnp.sum(jnp.where(self.diag, column, 0.0), axis=0, keepdims=True)

    def to_column(self, line):
        return jnp.sum(jnp.where(self.diag, line, 0.0), axis=1, keepdims=True)


def gates(grid, betas_ref, decays_ref, h, c):
    pair, half = c // 2, C * (c % 2)
    lanes = pl.ds(pair * N, N)
    first = betas_ref[0, pl.ds(h, 1), lanes]
    second = betas_ref[1, pl.ds(h, 1), lanes]
    logs = jnp.log(decays_ref[pl.ds(h, 1), lanes])
    offset = grid.lane - half
    chosen = jnp.where(grid.row < C, first, second)
    beta = jnp.sum(jnp.where(offset == grid.row_pos, chosen, 0.0), axis=1, keepdims=True)
    seen = (offset >= 0) & (offset <= grid.row_pos)
    run = jnp.sum(jnp.where(seen, logs, 0.0), axis=1, keepdims=True)
    inside = (offset[:1] >= 0) & (offset[:1] < C)
    end = jnp.sum(jnp.where(inside, logs, 0.0), axis=1, keepdims=True)
    return beta, run, grid.to_row(run), end


def pair_rows(ref, heads, h, c):
    base = c * C * 2 * heads
    return jnp.concatenate(
        [
            ref[pl.ds(base + h, C, stride=2 * heads), :],
            ref[pl.ds(base + heads + h, C, stride=2 * heads), :],
        ],
        axis=0,
    )


BETA, READ, TAIL, SCALE = range(4)


def pair_product(ah, al, bh, bl):
    wide = jnp.concatenate([bh, bl], axis=1)
    both = contract(jnp.concatenate([ah, al], axis=1), jnp.concatenate([wide, wide], axis=0), 1, 0)
    half = bh.shape[1]
    return both[:, :half] + both[:, half:]


def local_kernel(heads, count, dk_ref, dv_ref, betas_ref, decays_ref,
                 k_ref, kt_ref, inv_ref, p_ref, y_ref, t_ref, o_ref, fade_ref, see_ref, run_ref, col_ref,
                 tsh_ref, osh_ref, low_ref,
                 keys_scr, values_scr, sys_scr, split_scr, half_scr, rhs_scr):
    grid = Grid()
    eye = jnp.where(grid.diag, 1.0, 0.0)
    items = [(h, c) for h in range(heads) for c in range(count)]
    keys_scr[...] = dk_ref[...].astype(F32)
    values_scr[...] = dv_ref[...].astype(F32)
    ends = {}
    for h, c in items:
        raw = pair_rows(keys_scr, heads, h, c)
        values = pair_rows(values_scr, heads, h, c)
        scale = lax.rsqrt(jnp.sum(raw * raw, axis=1, keepdims=True) + EPS)
        keys = raw * scale
        beta, run, line, end = gates(grid, betas_ref, decays_ref, h, c)
        tail = jnp.exp(end - run)
        read = beta * jnp.exp(run)
        fade = beta * jnp.where(grid.strict, jnp.exp(jnp.minimum(run - line, 0.0)), 0.0)
        seen = grid.lane_pos[:C] <= grid.row_pos[:C]
        see_ref[h, c] = jnp.where(seen, jnp.exp(jnp.minimum(run[:C] - line, 0.0)), 0.0)
        run_ref[h, c] = jnp.broadcast_to(jnp.exp(run[:C]), (C, N))
        col_ref[h, c] = jnp.where(
            grid.lane == BETA, beta,
            jnp.where(grid.lane == READ, read, jnp.where(grid.lane == TAIL, tail, scale)),
        )
        k_ref[h, c] = keys
        kt_ref[h, c] = keys * tail
        fade_ref[h, c] = fade
        system = fade * mm_nt(keys, keys)
        sys_scr[0, h, c], sys_scr[1, h, c] = split(system)
        inverse = eye - jnp.where(grid.differ == 1, system, 0.0)
        inv_ref[h, c] = inverse
        split_scr[0, h, c], split_scr[1, h, c] = split(inverse)
        rhs_scr[h, c, :, :N] = read * keys
        rhs_scr[h, c, :, N:] = beta * values
        ends[h, c] = jnp.exp(end)
    for level in range(1, 7):
        near = (grid.differ >= (1 << level)) & (grid.differ < (2 << level))
        near = jnp.where(near, 1.0, 0.0).astype(BF16)
        for h, c in items:
            half = pair_product(
                sys_scr[0, h, c] * near, sys_scr[1, h, c] * near, split_scr[0, h, c], split_scr[1, h, c]
            )
            half_scr[0, h, c], half_scr[1, h, c] = split(half)
        for h, c in items:
            inverse = inv_ref[h, c] - pair_product(
                split_scr[0, h, c], split_scr[1, h, c], half_scr[0, h, c], half_scr[1, h, c]
            )
            inv_ref[h, c] = inverse
            split_scr[0, h, c], split_scr[1, h, c] = split(inverse)
    for h, c in items:
        both = pair_product(split_scr[0, h, c], split_scr[1, h, c], *split(rhs_scr[h, c]))
        p_ref[h, c] = both[:, :N]
        y_ref[h, c] = both[:, N:]
    for i in items:
        maps = mm_tn(kt_ref[i], jnp.concatenate([p_ref[i], y_ref[i]], axis=1))
        t_ref[i] = ends[i] * eye - maps[:, :N]
        o_ref[i] = maps[:, N:]
    for h in range(heads):
        tsh_ref[h] = t_ref[h, 0]
        osh_ref[h] = o_ref[h, 0]
    for c in range(1, count):
        for h in range(heads):
            both = mm(t_ref[h, c], jnp.concatenate([tsh_ref[h], osh_ref[h]], axis=1))
            tsh_ref[h] = both[:, :N]
            osh_ref[h] = both[:, N:] + o_ref[h, c]
    for h in range(heads):
        low_ref[0, h] = osh_ref[h].astype(BF16)
        low_ref[1, h] = tsh_ref[h].astype(BF16)


def gather_blocks(place_ref, refs, scr):
    count = len(refs)
    for s in range(count):
        scr[lax.rem(place_ref[0] + count - s, count)] = refs[s][...]


def scatter_blocks(place_ref, scr, refs):
    count = len(refs)
    for s in range(count):
        refs[s][...] = scr[lax.rem(place_ref[0] + s, count)]


def head_rows(ref, heads, h, c):
    return ref[pl.ds(c * C * heads + h, C, stride=heads), :]


def readout_kernel(heads, count, place_ref, g_ref, near_ref, far_ref, k_ref, p_ref, y_ref, t_ref, o_ref, see_ref, run_ref,
                   s_ref, u_ref, dw_ref, dq_ref, *rest):
    outs, (g_scr, dq_scr) = rest[:heads], rest[heads:]
    g_scr[...] = g_ref[...].astype(F32)
    for h in range(heads):
        s_ref[h, 0] = near_ref[0, h].astype(F32) + contract(near_ref[1, h], far_ref[h], 1, 0)
    for c in range(count):
        for h in range(heads):
            both = mm(jnp.concatenate([t_ref[h, c], p_ref[h, c]], axis=0), s_ref[h, c])
            u_ref[h, c] = y_ref[h, c] - both[N:]
            s_ref[h, c + 1] = both[:N] + o_ref[h, c]
    items = [(h, c) for h in range(heads) for c in range(count)]
    for h, c in items:
        cot = head_rows(g_scr, heads, h, c).astype(BF16)
        both = low_nt(cot, jnp.concatenate([u_ref[h, c], s_ref[h, c]], axis=0))
        dw_ref[h, c] = both[:, :N] * see_ref[h, c]
        dq_ref[h, c] = run_ref[h, c] * both[:, N:]
    for h, c in items:
        grad = mm(dw_ref[h, c], k_ref[h, c]) + dq_ref[h, c]
        dq_ref[h, c] = grad
        dq_scr[h, pl.ds(c * C, C), :] = grad.astype(BF16)
    scatter_blocks(place_ref, dq_scr, outs)


def unit_queries(low):
    raw = low.astype(F32)
    return raw * lax.rsqrt(jnp.mean(raw * raw, axis=1, keepdims=True) + EPS)


def source_kernel(heads, count, place_ref, g_ref, k_ref, p_ref, t_ref, see_ref, run_ref, map_ref, *rest):
    ins, (q_ref, z_ref, b_ref, bsh_ref, low_ref, g_scr, q_scr) = rest[:heads], rest[heads:]
    gather_blocks(place_ref, ins, q_scr)
    g_scr[...] = g_ref[...].astype(F32)
    items = [(h, c) for h in range(heads) for c in range(count)]
    weights = {}
    for h, c in items:
        query = unit_queries(q_scr[h, pl.ds(c * C, C), :])
        q_ref[h, c] = query
        weights[h, c] = mm_nt(query, k_ref[h, c]) * see_ref[h, c]
    for h, c in items:
        cot = head_rows(g_scr, heads, h, c).astype(BF16)
        z_ref[h, c] = low_tn(weights[h, c], cot)
        b_ref[h, c] = low_tn(q_ref[h, c] * run_ref[h, c], cot)
    for h, c in items:
        b_ref[h, c] = b_ref[h, c] - mm_tn(p_ref[h, c], z_ref[h, c])
    for h in range(heads):
        bsh_ref[h] = b_ref[h, count - 1]
    for c in range(count - 2, -1, -1):
        for h in range(heads):
            bsh_ref[h] = b_ref[h, c] + mm_tn(t_ref[h, c], bsh_ref[h])
    for h in range(heads):
        low_ref[0, h] = bsh_ref[h].astype(BF16)
        low_ref[1, h] = map_ref[1, h]


def final_kernel(heads, count, decays_ref, near_ref, far_ref, k_ref, kt_ref, inv_ref, t_ref, fade_ref, col_ref,
                 s_ref, u_ref, dw_ref, dq_ref, q_ref, z_ref, b_ref,
                 gk_ref, gv_ref, gb_ref, gd_ref, gk_scr, gv_scr, lam_scr, r_scr, d_scr, rd_scr):
    grid = Grid()
    items = [(h, c) for h in range(heads) for c in range(count)]
    for h in range(heads):
        lam_scr[h, count - 1] = near_ref[0, h].astype(F32) + contract(near_ref[1, h], far_ref[h], 0, 0)
    for c in range(count - 1, 0, -1):
        for h in range(heads):
            lam_scr[h, c - 1] = mm_tn(t_ref[h, c], lam_scr[h, c]) + b_ref[h, c]
    for i in items:
        d_scr[i] = z_ref[i] + mm(kt_ref[i], lam_scr[i])
    for i in items:
        r_scr[i] = mm_tn(inv_ref[i], d_scr[i])
    for h, c in items:
        both = mm_nt(r_scr[h, c], jnp.concatenate([u_ref[h, c], s_ref[h, c]], axis=0))
        d_scr[h, c] = -both[:, :N] * fade_ref[h, c]
        rd_scr[h, c] = -col_ref[h, c, :, READ:READ + 1] * both[:, N:]
    lines = {}
    for h, c in items:
        keys, r = k_ref[h, c], r_scr[h, c]
        cols = col_ref[h, c]
        beta, tail, scale = (cols[:, n:n + 1] for n in (BETA, TAIL, SCALE))
        gb = jnp.sum(r * u_ref[h, c], axis=1, keepdims=True) / beta
        read = mm(d_scr[h, c], keys) + rd_scr[h, c]
        query = q_ref[h, c]
        write = mm_tn(d_scr[h, c], keys) + tail * mm_nt(u_ref[h, c], lam_scr[h, c]) + mm_tn(dw_ref[h, c], query)
        grad = read + write
        gk = scale * (grad - keys * jnp.sum(keys * grad, axis=1, keepdims=True))
        gv = beta * r
        base = c * C * 2 * heads
        for m in range(2):
            rows = pl.ds(base + m * heads + h, C, stride=2 * heads)
            gk_scr[rows, :] = gk[m * C:(m + 1) * C]
            gv_scr[rows, :] = gv[m * C:(m + 1) * C]
        pulls = keys * (read - write)
        pulls = jnp.sum(pulls[:C] + pulls[C:] + query * dq_ref[h, c], axis=1, keepdims=True)
        after = grid.row_pos[:C] >= grid.lane_pos[:C]
        total = jnp.sum(
            jnp.sum(s_ref[h, c + 1] * lam_scr[h, c], axis=0, keepdims=True), axis=1, keepdims=True
        )
        gd = jnp.sum(jnp.where(after, pulls, 0.0), axis=0, keepdims=True) + total
        half = C * (c % 2)
        mine = (grid.lane[:1] >= half) & (grid.lane[:1] < half + C)
        lines[h, c, 2] = jnp.where(mine, gd, 0.0)
        for m in range(2):
            pick = (grid.lane - half == grid.row - m * C) & (grid.row >= m * C) & (grid.row < (m + 1) * C)
            lines[h, c, m] = jnp.sum(jnp.where(pick, gb, 0.0), axis=0, keepdims=True)
    for h in range(heads):
        for p in range(count // 2):
            lanes = pl.ds(p * N, N)
            for m in range(2):
                gb_ref[m, pl.ds(h, 1), lanes] = lines[h, 2 * p, m] + lines[h, 2 * p + 1, m]
            gd_ref[pl.ds(h, 1), lanes] = (lines[h, 2 * p, 2] + lines[h, 2 * p + 1, 2]) / decays_ref[pl.ds(h, 1), lanes]
    gk_ref[...] = gk_scr[...].astype(BF16)
    gv_ref[...] = gv_scr[...].astype(BF16)


HBM = pl.BlockSpec(memory_space=pltpu.HBM)
SCALAR = pl.BlockSpec(memory_space=pltpu.SMEM)
VM = pl.BlockSpec(memory_space=pltpu.VMEM)


def shaped(shape, dtype=F32):
    return jax.ShapeDtypeStruct(shape, dtype)


def single(body, name, in_specs, outs, out_specs, scratch, flops, limit=LIMIT):
    return pl.pallas_call(
        body,
        name=name,
        in_specs=in_specs,
        out_shape=outs,
        out_specs=out_specs,
        scratch_shapes=scratch,
        compiler_params=pltpu.CompilerParams(vmem_limit_bytes=limit),
        cost_estimate=pl.CostEstimate(flops=flops, bytes_accessed=4 << 20, transcendentals=0),
    )


def delta_local(dk, dv, betas, decays):
    heads, rows = decays.shape
    count = rows // C
    square, thin, one = (shaped((heads,) + tail) for tail in ((count, N, N), (count, C, N), (N, N)))
    outs = [square] * 8 + [thin] * 2 + [square] + [one] * 2 + [shaped((2, heads, N, N), BF16)]
    halves = pltpu.VMEM((2, heads, count, N, N), BF16)
    return single(
        functools.partial(local_kernel, heads, count), "delta_local",
        [VM] * 4, outs, [VM] * len(outs),
        [pltpu.VMEM(dk.shape, F32)] * 2 + [halves] * 3
        + [pltpu.VMEM((heads, count, N, 2 * N), F32)],
        10 << 30,
    )(dk, dv, betas, decays)


def delta_readout(place, g, near, far, k, p, y, t, o, see, run):
    heads, count = k.shape[:2]
    rows = count * C
    square, thin = (shaped((heads,) + tail) for tail in ((count, N, N), (count, C, N)))
    outs = [shaped((heads, count + 1, N, N)), square, thin, thin]
    return single(
        functools.partial(readout_kernel, heads, count), "delta_readout",
        [SCALAR] + [VM] * 10, outs + [shaped((rows, N), BF16)] * heads, [VM] * (4 + heads),
        [pltpu.VMEM(g.shape, F32), pltpu.VMEM((heads, rows, N), BF16)],
        3 << 30,
    )(place, g, near, far, k, p, y, t, o, see, run)


def delta_source(place, g, k, p, t, see, run, low, attended):
    heads, count = k.shape[:2]
    rows = count * C
    square, thin = (shaped((heads,) + tail) for tail in ((count, N, N), (count, C, N)))
    return single(
        functools.partial(source_kernel, heads, count), "delta_source",
        [SCALAR] + [VM] * (7 + heads),
        [thin, square, square, shaped((heads, N, N)), shaped(low.shape, BF16)], [VM] * 5,
        [pltpu.VMEM(g.shape, F32), pltpu.VMEM((heads, rows, N), BF16)],
        3 << 30,
    )(place, g, k, p, t, see, run, low, *attended)


def delta_final(betas, decays, near, far, k, kt, inv, t, fade, col, s, u, dw, dq, q, z, b):
    heads, count = k.shape[:2]
    wide = (2 * count * C * heads, N)
    return single(
        functools.partial(final_kernel, heads, count), "delta_final",
        [VM] * 16,
        [shaped(wide, BF16), shaped(wide, BF16), shaped(betas.shape), shaped(decays.shape)], [VM] * 4,
        [pltpu.VMEM(wide, F32)] * 2 + [pltpu.VMEM((heads, count, N, N), F32)] * 4,
        8 << 30,
    )(decays, near, far, k, kt, inv, t, fade, col, s, u, dw, dq, q, z, b)


def rounds(refs, index, count, sign):
    return [lax.rem(index + (s if sign > 0 else count - s), count) for s in range(count)]


def send_kernel(count, place_ref, q_ref, k_ref, v_ref, *rest):
    outs, (low, scr, sem) = rest[:count], rest[count:]
    heads = count
    rows = q_ref.shape[0] // heads
    copies = [pltpu.make_async_copy(ref, low.at[m], sem.at[m]) for m, ref in enumerate((q_ref, k_ref, v_ref))]
    for copy in copies:
        copy.start()
    for m in range(3):
        copies[m].wait()
        scr[m] = low[m].astype(F32)
        for s in range(count):
            head = lax.rem(place_ref[0] + s, count)
            outs[s][m] = scr[m, pl.ds(head, rows, stride=heads), :].astype(BF16)


def take_kernel(count, place_ref, *rest):
    ins, outs, (scr, low, sem) = rest[:count], rest[count:count + 3], rest[count + 3:]
    heads = count
    rows = low.shape[1] // heads
    copies = []
    for m in range(3):
        for s in range(count):
            head = lax.rem(place_ref[0] + count - s, count)
            scr[m, pl.ds(head, rows, stride=heads), :] = ins[s][m].astype(F32)
        low[m] = scr[m].astype(BF16)
        copies.append(pltpu.make_async_copy(low.at[m], outs[m], sem.at[m]))
        copies[m].start()
    for copy in copies:
        copy.wait()


def attend_kernel(count, scale, place_ref, *rest):
    ins, (whole_ref, prob_ref, mixed_ref), outs = rest[:count], rest[count:count + 3], rest[count + 3:2 * count + 3]
    (att_scr,) = rest[2 * count + 3:]
    gather_blocks(place_ref, ins, whole_ref)
    rows = whole_ref.shape[2]
    causal = iota((rows, rows), 0) <= iota((rows, rows), 1)
    for i in range(count):
        query = whole_ref[i, 0]
        pieces = []
        for j in range(i + 1):
            score = contract(whole_ref[j, 1], query, 1, 1) * scale
            pieces.append(jnp.where(causal, score, -jnp.inf) if j == i else score)
        top = pieces[0].max(axis=0, keepdims=True)
        for piece in pieces[1:]:
            top = jnp.maximum(top, piece.max(axis=0, keepdims=True))
        pieces = [jnp.exp(piece - top) for piece in pieces]
        total = pieces[0].sum(axis=0, keepdims=True)
        for piece in pieces[1:]:
            total = total + piece.sum(axis=0, keepdims=True)
        share = 1.0 / total
        mixed = None
        for j, piece in enumerate(pieces):
            low = (piece * share).astype(BF16)
            prob_ref[i * (i + 1) // 2 + j] = low
            term = contract(low, whole_ref[j, 2], 0, 0)
            mixed = term if mixed is None else mixed + term
        mixed_ref[i] = mixed
        att_scr[i] = mixed.astype(BF16)
    scatter_blocks(place_ref, att_scr, outs)


def attend_back_kernel(count, scale, place_ref, prob_ref, mixed_ref, whole_ref, *rest):
    grads, outs = rest[:count], rest[count:2 * count]
    g_scr, out_scr, acc = rest[2 * count:]
    gather_blocks(place_ref, grads, g_scr)
    rows = whole_ref.shape[2]
    ones = jnp.ones((8, N), F32)
    for i in range(count - 1, -1, -1):
        mixed = mixed_ref[i]
        low = mixed.astype(BF16).astype(F32)
        grad = g_scr[i].astype(F32)
        inv = lax.rsqrt(jnp.mean(low * low, axis=1, keepdims=True) + EPS)
        pull = inv * (grad - low * (inv * inv * jnp.mean(low * grad, axis=1, keepdims=True)))
        pull = pull.astype(BF16)
        dots = mm_nt(ones, pull.astype(F32) * mixed)[:1]
        query = whole_ref[i, 0]
        gq = None
        for j in range(i + 1):
            prob = prob_ref[i * (i + 1) // 2 + j]
            gp = contract(whole_ref[j, 2], pull, 1, 1)
            gs = (prob.astype(F32) * (gp - dots) * scale).astype(BF16)
            term = contract(gs, whole_ref[j, 1], 0, 0)
            gq = term if gq is None else gq + term
            gk = contract(gs, query, 1, 0)
            gv = contract(prob, pull, 1, 0)
            if i < count - 1:
                gk, gv = gk + acc[j, 0], gv + acc[j, 1]
            if i == j:
                out_scr[j, 1] = gk.astype(BF16)
                out_scr[j, 2] = gv.astype(BF16)
            else:
                acc[j, 0] = gk
                acc[j, 1] = gv
        out_scr[i, 0] = gq.astype(BF16)
    scatter_blocks(place_ref, out_scr, outs)


def send_heads(place, q, k, v, count):
    rows = q.shape[0] // count
    return single(
        functools.partial(send_kernel, count), "send_heads",
        [SCALAR, HBM, HBM, HBM], [shaped((3, rows, N), BF16)] * count, [VM] * count,
        [pltpu.VMEM((3,) + q.shape, BF16), pltpu.VMEM((3,) + q.shape, F32), pltpu.SemaphoreType.DMA((3,))],
        SENDFLOPS, SENDLIMIT,
    )(place, q, k, v)


def take_heads(place, parts):
    count = len(parts)
    rows = parts[0].shape[1]
    wide = (rows * count, N)
    return single(
        functools.partial(take_kernel, count), "take_heads",
        [SCALAR] + [VM] * count, [shaped(wide, BF16)] * 3, [HBM] * 3,
        [pltpu.VMEM((3,) + wide, F32), pltpu.VMEM((3,) + wide, BF16), pltpu.SemaphoreType.DMA((3,))], 1 << 28,
    )(place, *parts)


def attend(place, parts, scale):
    count = len(parts)
    rows = parts[0].shape[1]
    tri = count * (count + 1) // 2
    return single(
        functools.partial(attend_kernel, count, scale), "attend",
        [SCALAR] + [VM] * count,
        [shaped((count, 3, rows, N), BF16), shaped((tri, rows, rows), BF16), shaped((count, rows, N))]
        + [shaped((rows, N), BF16)] * count,
        [VM] * (3 + count),
        [pltpu.VMEM((count, rows, N), BF16)], 2 << 30,
    )(place, *parts)


def attend_back(place, prob, mixed, whole, grads, scale):
    count, _, rows, _ = whole.shape
    return single(
        functools.partial(attend_back_kernel, count, scale), "attend_back",
        [SCALAR] + [VM] * (3 + count),
        [shaped((3, rows, N), BF16)] * count, [VM] * count,
        [pltpu.VMEM((count, rows, N), BF16), pltpu.VMEM((count, 3, rows, N), BF16),
         pltpu.VMEM((count, 2, rows, N), F32)], 4 << 30,
    )(place, prob, mixed, whole, *grads)


PRECISE = lax.Precision.HIGHEST


def shifted(value, axis, steps):
    count = lax.axis_size(axis)
    initial, last = (max(0, -steps), min(count, count - steps))
    return lax.ppermute(value, axis, [(source, source + steps) for source in range(initial, last)])


def rotated(parts, axis):
    count = len(parts)
    moved = [parts[0]]
    for s in range(1, count):
        moved.append(lax.ppermute(parts[s], axis, [(d, (d + s) % count) for d in range(count)]))
    return moved


def apply_map(matrix, state):
    return jnp.einsum("hij,hjk->hik", matrix, state, precision=PRECISE)


def entering(low, matrix, offset, axis, step):
    count = lax.axis_size(axis)
    if count <= 4:
        near = shifted(low, axis, step)
        middle = (apply_map(matrix, near[0].astype(F32)) + offset).astype(BF16)
        return near, shifted(middle, axis, 2 * step), middle
    place = lax.axis_index(axis)
    place = place if step > 0 else count - 1 - place
    eye = jnp.eye(matrix.shape[-1], dtype=F32)
    reach = 1
    while reach < count:
        before, start = (shifted(matrix, axis, step * reach), shifted(offset, axis, step * reach))
        before = before + jnp.where(place < reach, eye, 0.0)
        offset = apply_map(matrix, start) + offset
        matrix = apply_map(matrix, before)
        reach *= 2
    state = shifted(offset, axis, step).astype(BF16)
    return jnp.stack([state, jnp.zeros_like(state)]), jnp.zeros_like(state), state


def visible_pairs(rows, span):
    relative = jnp.arange((span + 1) * rows, dtype=jnp.int32) - span * rows
    local = jnp.arange(rows, dtype=jnp.int32)
    return (
        (relative[None, :] <= local[:, None])
        & (relative[None, :] > local[:, None] - WINDOW)
        & (lax.axis_index("seq") * rows + relative[None, :] >= 0)
    )


def window_forward(queries, keys, values, scale):
    rows = queries.shape[0]
    span = -(-WINDOW // rows)
    couple = jnp.stack([keys, values])
    earlier = [shifted(couple, "seq", step + 1) for step in range(min(span, lax.axis_size("seq") - 1))]
    span = len(earlier)
    ordered = earlier[::-1] + [couple]
    window_keys = jnp.concatenate([piece[0] for piece in ordered], axis=0)
    window_values = jnp.concatenate([piece[1] for piece in ordered], axis=0)
    visible = visible_pairs(rows, span)
    scores = jnp.einsum("qhe,khe->hqk", queries, window_keys, preferred_element_type=F32) * scale
    top = jnp.max(jnp.where(visible, scores, -jnp.inf), axis=-1)
    lifted = jnp.where(visible, jnp.exp(jnp.where(visible, scores - top[:, :, None], 0.0)), 0.0)
    attention = lifted / jnp.sum(lifted, axis=-1)[:, :, None]
    mixed = jnp.einsum(
        "hqk,khe->qhe", attention.astype(BF16), window_values, preferred_element_type=F32
    )
    return window_keys, window_values, attention, mixed, span


def window_backward(queries, window_keys, window_values, attention, mixed, span, unit_grad, scale):
    rows = queries.shape[0]
    low = mixed.astype(BF16).astype(F32)
    grad = unit_grad.astype(F32)
    inv = lax.rsqrt(jnp.mean(low * low, axis=-1, keepdims=True) + EPS)
    pull = inv * (grad - low * (inv * inv * jnp.mean(low * grad, axis=-1, keepdims=True)))
    pull = pull.astype(BF16)
    row_dots = jnp.sum(pull.astype(F32) * mixed, axis=-1).T
    grad_attention = jnp.einsum("qhe,khe->hqk", pull, window_values, preferred_element_type=F32)
    grad_scores = (attention * (grad_attention - row_dots[:, :, None]) * scale).astype(BF16)
    grad_queries = jnp.einsum(
        "hqk,khe->qhe", grad_scores, window_keys, preferred_element_type=F32
    ).astype(BF16)
    key_parts = jnp.einsum("hqk,qhe->khe", grad_scores, queries, preferred_element_type=F32)
    value_parts = jnp.einsum("hqk,qhe->khe", attention.astype(BF16), pull, preferred_element_type=F32)
    gathered = jnp.stack([key_parts[span * rows:], value_parts[span * rows:]])
    for later in range(1, span + 1):
        first = (span - later) * rows
        piece = jnp.stack([key_parts[first:first + rows], value_parts[first:first + rows]])
        gathered = gathered + shifted(piece, "seq", -later)
    return grad_queries, gathered[0].astype(BF16), gathered[1].astype(BF16)


def body(queries, keys, values, delta_keys, delta_values, betas, decays, grad_out):
    rows, heads, width = queries.shape
    scale = 1.0 / math.sqrt(width)
    count = lax.axis_size("seq")
    by_head = heads == count and WINDOW >= count * rows

    def flat(array):
        return array.reshape(-1, width)

    place = lax.axis_index("seq").astype(jnp.int32).reshape(1) if by_head else jnp.zeros((1,), jnp.int32)
    extra = (flat(delta_keys), flat(delta_values), betas, decays)
    if by_head:
        parts = send_heads(place, flat(queries), flat(keys), flat(values), count)
        first, parts = lax.optimization_barrier((extra[0], parts))
        extra = (first,) + extra[1:]
        parts = rotated(parts, "seq")
    cot = flat(grad_out)
    k, kt, inverse, p, y, t, o, fade, see, run, col, shard_t, shard_o, low = delta_local(*extra)
    near, far, middle = entering(low, shard_t, shard_o, "seq", 1)
    if by_head:
        whole, prob, mixed, *attended = attend(place, parts, scale)
        attended = rotated(attended, "seq")
    else:
        saved = window_forward(queries, keys, values, scale)
        rounded = saved[3].astype(BF16)
        attended = [rounded[:, (heads - s) % heads] for s in range(heads)]
    s, u, dw, dq, *pulls = delta_readout(place, cot, near, far, k, p, y, t, o, see, run)
    if by_head:
        pulls = rotated(pulls, "seq")
        outs = rotated(attend_back(place, prob, mixed, whole, pulls, scale), "seq")
    else:
        grads = window_backward(queries, *saved, jnp.stack(pulls, axis=1), scale)
    attended, _ = lax.optimization_barrier((attended, middle))
    q, z, b, shard_source, low = delta_source(place, cot, k, p, t, see, run, low, attended)
    near, far, _ = entering(low, jnp.swapaxes(shard_t, 1, 2), shard_source, "seq", -1)
    grad_keys, grad_values, grad_betas, grad_decays = delta_final(
        betas, decays, near, far, k, kt, inverse, t, fade, col, s, u, dw, dq, q, z, b
    )
    if by_head:
        outs, grad_keys = lax.optimization_barrier((outs, grad_keys))
        grads = [array.reshape(rows, heads, width) for array in take_heads(place, outs)]
    pair = (rows, 2, heads, width)
    return (*grads, grad_keys.reshape(pair), grad_values.reshape(pair), grad_betas, grad_decays)


def solution(mesh):
    row = P(("parts", "seq"), "head", None)
    pair = P(("parts", "seq"), None, "head", None)
    beta = P(None, "head", ("parts", "seq"))
    decay = P("head", ("parts", "seq"))
    return jax.shard_map(
        body,
        mesh=mesh,
        in_specs=(row, row, row, pair, pair, beta, decay, row),
        out_specs=(row, row, row, pair, pair, beta, decay),
        check_vma=False,
    )
```
